32 devices in a mesh: shard: 2 (over y), ctx: 4 (over x, core), tp: 4 (over z).
Axes of the slice: x: 2, y: 2, z: 4, core: 2. Of those that a mesh axis runs over, the one named last changes fastest.
Arguments:
- tokens: bfloat16 [4, 4096, 768], P('shard', ('ctx', 'tp')), may hold values from -6 to 6
- cotangent: bfloat16 [4, 4096, 768], P('shard', ('ctx', 'tp')), may hold values from -6 to 6
- lengths: int32 [4], P('shard'), may hold values from 1024 to 4096, as said below
- query_weight: bfloat16 [768, 768], P('shard', 'tp'), may hold values from -0.4375 to 0.4375
- query_bias: float32 [768], P('tp'), may hold values from -3 to 3
- key_weight: bfloat16 [768, 768], P('shard', 'tp'), may hold values from -0.21875 to 0.21875
- value_weight: bfloat16 [768, 768], P('shard', 'tp'), may hold values from -0.21875 to 0.21875
- value_bias: float32 [768], P('tp'), may hold values from -3 to 3
- out_weight: bfloat16 [768, 768], P('tp', 'shard'), may hold values from -1.75 to 1.75
- out_bias: float32 [768], replicated, may hold values from -3 to 3
- first_gain: float32 [768], replicated, may hold values from 0.1 to 1.9
- first_shift: float32 [768], replicated, may hold values from -3 to 3
- up_weight: bfloat16 [768, 3072], P('shard', 'tp'), may hold values from -0.21875 to 0.21875
- up_bias: float32 [3072], P('tp'), may hold values from -3 to 3
- down_weight: bfloat16 [3072, 768], P('tp', 'shard'), may hold values from -0.109375 to 0.109375
- down_bias: float32 [768], replicated, may hold values from -3 to 3
- second_gain: float32 [768], replicated, may hold values from 0.1 to 1.9
- second_shift: float32 [768], replicated, may hold values from -3 to 3
Outputs:
- output: bfloat16 [4, 4096, 768], P('shard', ('ctx', 'tp'))
- input_grad: bfloat16 [4, 4096, 768], P('shard', ('ctx', 'tp'))
- query_weight_grad: float32 [768, 768], P('shard', 'tp')
- query_bias_grad: float32 [768], replicated
- key_weight_grad: float32 [768, 768], P('shard', 'tp')
- value_weight_grad: float32 [768, 768], P('shard', 'tp')
- value_bias_grad: float32 [768], replicated
- out_weight_grad: float32 [768, 768], P('tp', 'shard')
- out_bias_grad: float32 [768], replicated
- first_gain_grad: float32 [768], replicated
- first_shift_grad: float32 [768], replicated
- up_weight_grad: float32 [768, 3072], P('shard', 'tp')
- up_bias_grad: float32 [3072], replicated
- down_weight_grad: float32 [3072, 768], P('tp', 'shard')
- down_bias_grad: float32 [768], replicated
- second_gain_grad: float32 [768], replicated
- second_shift_grad: float32 [768], replicated
The draws below stay inside these ranges and needn't reach their ends.
Inputs may be any that keep to these rules, and one draw needn't show every extreme that they name: `lengths`: positions below a sequence's length are its tokens, the rest padding; some sequence has exactly 4096 valid positions and some exactly 1024.
All inputs are finite; a program needn't handle non-finite values.
Results may differ from the reference program's by a relative error of at most 0.023.
Values may be sent and summed in bfloat16 or wider, within the bound.
No kernel may reach another device: no remote copies, remote signals or barrier semaphores. Data moves between devices by JAX's collectives and lax.ppermute only.
A program may use at most 128 MiB of HBM per device.

```python
import jax
import jax.numpy as jnp
from jax import lax

D = 768
HEADS = 12
HD = 64
FF = 3072
LEN = 4096
SEQS = 4


def draw_lengths(key, part):
    first_key, second_key = jax.random.split(key)
    drawn = jax.random.randint(first_key, (SEQS,), LEN // 4, LEN + 1)
    order = jax.random.permutation(second_key, SEQS)
    drawn = drawn.at[order[0]].set(LEN)
    drawn = drawn.at[order[1]].set(LEN // 4)
    return drawn.astype(jnp.int32)


def block_levels(stream_key, dims, pieces, least, high):
    def one(position, blocks):
        draws = jax.random.uniform(jax.random.fold_in(jax.random.fold_in(stream_key, 6), position), (blocks,), jnp.float32, least / len(pieces), high / len(pieces))
        return jnp.repeat(jnp.exp(draws), dims[position] // blocks).reshape((-1,) + (1,) * (len(dims) - position - 1))

    level = one(*pieces[0])
    for cut in pieces[1:]:
        level = level * one(*cut)
    return level


def bell_draw(rng, extent, spread, most, cuts=(), held_as=jnp.bfloat16):
    values = jax.random.normal(rng, extent, jnp.float32) * spread
    if len(cuts) > 0:
        values = block_levels(rng, extent, cuts, -0.22, 0.18) * values
    return jnp.clip(values, min=-most, max=most).astype(held_as)


def setup_inputs(seed: int = 0) -> dict:
    key_of = jax.random.split(jax.random.key(seed), 19)
    tokens = bell_draw(key_of[0], (SEQS, LEN, D), 1.0, 6.0, ((0, 2), (1, 16)))
    cotangent = bell_draw(key_of[1], (SEQS, LEN, D), 1.0, 6.0, ((0, 2), (1, 16)))
    lengths = draw_lengths(jax.random.fold_in(key_of[18], 71), 0)
    query_weight = bell_draw(key_of[3], (D, D), (D // 4) ** -0.5, 0.4375, ((0, 2), (1, 4)))
    query_bias = bell_draw(key_of[4], (D,), 0.5, 3.0, ((0, 4),), jnp.float32)
    key_weight = bell_draw(key_of[5], (D, D), D ** -0.5, 0.21875, ((0, 2), (1, 4)))
    value_weight = bell_draw(key_of[6], (D, D), D ** -0.5, 0.21875, ((0, 2), (1, 4)))
    value_bias = bell_draw(key_of[7], (D,), 0.5, 3.0, ((0, 4),), jnp.float32)
    out_weight = bell_draw(key_of[8], (D, D), (D // 64) ** -0.5, 1.75, ((0, 4), (1, 2)))
    out_bias = bell_draw(key_of[9], (D,), 0.5, 3.0, (), jnp.float32)
    first_gain = jnp.clip(1.0 + 0.18 * jax.random.normal(key_of[10], (D,), jnp.float32), 0.1, 1.9)
    first_shift = bell_draw(key_of[11], (D,), 0.5, 3.0, (), jnp.float32)
    up_weight = bell_draw(key_of[12], (D, FF), D ** -0.5, 0.21875, ((0, 2), (1, 4)))
    up_bias = bell_draw(key_of[13], (FF,), 0.5, 3.0, ((0, 4),), jnp.float32)
    down_weight = bell_draw(key_of[14], (FF, D), FF ** -0.5, 0.109375, ((0, 4), (1, 2)))
    down_bias = bell_draw(key_of[15], (D,), 0.5, 3.0, (), jnp.float32)
    second_gain = jnp.clip(1.0 + 0.18 * jax.random.normal(key_of[16], (D,), jnp.float32), 0.1, 1.9)
    second_shift = bell_draw(key_of[17], (D,), 0.5, 3.0, (), jnp.float32)
    return dict(tokens=tokens, cotangent=cotangent, lengths=lengths, query_weight=query_weight, query_bias=query_bias, key_weight=key_weight, value_weight=value_weight, value_bias=value_bias, out_weight=out_weight, out_bias=out_bias, first_gain=first_gain, first_shift=first_shift, up_weight=up_weight, up_bias=up_bias, down_weight=down_weight, down_bias=down_bias, second_gain=second_gain, second_shift=second_shift)


@jax.custom_vjp
def low(v):
    return lax.optimization_barrier(v.astype(jnp.bfloat16)).astype(jnp.float32)

@jax.custom_vjp
def low_back(v):
    return v

def low_keep(v):
    return (low(v), None)

def low_pass(kept, grad):
    return (grad,)

def back_keep(v):
    return (v, None)

def back_low(kept, grad):
    return (low(grad),)
low.defvjp(low_keep, low_pass)
low_back.defvjp(back_keep, back_low)
highest = lax.Precision.HIGHEST
epsilon = 1e-12
masked_score = -1e+30

def matmul(left, right):
    return jnp.dot(left, right, precision=highest, preferred_element_type=jnp.float32)

def layer_norm(resid, gain, shift):
    centre = resid - lax.optimization_barrier(jnp.mean(resid, axis=-1, keepdims=True))
    factor = lax.rsqrt(lax.optimization_barrier(jnp.mean(centre * centre, axis=-1, keepdims=True)) + epsilon)
    return centre * factor * gain + shift

def encoder_layer(inputs, length, query_weight, query_bias, key_weight, value_weight, value_bias, out_weight, out_bias, first_gain, first_shift, up_weight, up_bias, down_weight, down_bias, second_gain, second_shift):
    seq_rows = inputs.shape[0]
    queries = low(low_back(matmul(inputs, query_weight) + query_bias)).reshape(seq_rows, HEADS, HD)
    keys = low(low_back(matmul(inputs, key_weight))).reshape(seq_rows, HEADS, HD)
    values = low(low_back(matmul(inputs, value_weight) + value_bias)).reshape(seq_rows, HEADS, HD)
    key_valid = (jnp.arange(seq_rows) < length)[None, None, :]
    block_rows = min(512, seq_rows)
    score_scale = HD ** (-0.5)

    def attend(query_block):
        scores = low_back(jnp.einsum('qhd,khd->hqk', query_block, keys, precision=highest) * score_scale)
        scores = jnp.where(key_valid, scores, masked_score)
        log_total = jax.nn.logsumexp(scores, axis=-1, keepdims=True)
        probs_low = low(jnp.exp(scores - log_total))
        return jnp.einsum('hqk,khd->qhd', probs_low, values, precision=highest)
    attended = lax.map(jax.checkpoint(attend), queries.reshape(seq_rows // block_rows, block_rows, HEADS, HD))
    attended = low(low_back(attended.reshape(seq_rows, HEADS * HD)))
    mixed = low_back(matmul(attended, out_weight) + out_bias)
    hidden = layer_norm(inputs + mixed, first_gain, first_shift)
    pre_act = low_back(matmul(low(hidden), up_weight) + up_bias)
    activated = low(jax.nn.gelu(pre_act, approximate=False))
    ffn_out = low_back(matmul(activated, down_weight) + down_bias)
    return layer_norm(hidden + ffn_out, second_gain, second_shift)

def reference(tokens, cotangent, lengths, query_weight, query_bias, key_weight, value_weight, value_bias, out_weight, out_bias, first_gain, first_shift, up_weight, up_bias, down_weight, down_bias, second_gain, second_shift):
    params = (query_weight, query_bias, key_weight, value_weight, value_bias, out_weight, out_bias, first_gain, first_shift, up_weight, up_bias, down_weight, down_bias, second_gain, second_shift)
    params = tuple((member.astype(jnp.float32) for member in params))

    def one_sequence(running, entries):
        inputs, grad_in, length = entries
        valid_rows = (jnp.arange(LEN) < length).astype(jnp.float32)[:, None]

        def layer_call(inputs_float, *weights):
            return encoder_layer(inputs_float, length, *weights)
        result, pull = jax.vjp(layer_call, inputs.astype(jnp.float32), *params)
        gradients = pull(grad_in.astype(jnp.float32) * valid_rows)
        running = tuple((before + update for before, update in zip(running, gradients[1:])))
        return (running, (result.astype(jnp.bfloat16), gradients[0].astype(jnp.bfloat16)))
    start_sums = tuple((jnp.zeros_like(member) for member in params))
    sums_final, (outputs, input_grads) = lax.scan(one_sequence, start_sums, (tokens, cotangent, lengths))
    return (outputs, input_grads, sums_final[0], sums_final[1], sums_final[2], sums_final[3], sums_final[4], sums_final[5], sums_final[6], sums_final[7], sums_final[8], sums_final[9], sums_final[10], sums_final[11], sums_final[12], sums_final[13], sums_final[14])
```

```python
import functools

import jax
import jax.numpy as jnp
from jax import lax
from jax.experimental import pallas as pl
from jax.experimental.pallas import tpu as pltpu
from jax.sharding import PartitionSpec as P

HD = 64
EXT = 128
VE = 80
epsilon = 1e-12
f32 = jnp.float32
bf16 = jnp.bfloat16


def extended(block, extra_rows):
    n = block.shape[1]
    row = lax.broadcasted_iota(jnp.int32, (EXT - HD, n), 0)
    extra = jnp.zeros((EXT - HD, n), f32)
    for place, values in enumerate(extra_rows):
        extra = jnp.where(row == place, values, extra)
    return jnp.concatenate([block, extra.astype(bf16)], axis=0)


def key_bias(meta, block, size, blocks):
    count = meta[1 + blocks + block]
    lane = lax.broadcasted_iota(jnp.int32, (1, size), 1)
    return jnp.where(lane < count, 0.0, -1e30).astype(f32)


def forward_kernel(meta, qt, *refs, size, pieces, inner, unroll):
    kv = refs[:pieces]
    ot, lse, key_rows, value_cols, acc, top = refs[pieces:]
    blocks = pieces * inner
    n = qt.shape[1]
    one = jnp.ones((1, size), f32)
    for e in range(pieces):
        for j in range(inner):
            b = e * inner + j
            here = slice(j * size, (j + 1) * size)
            there = slice(b * size, (b + 1) * size)
            bias = key_bias(meta, b, size, blocks)
            key_rows[there, :] = extended(kv[e][:HD, here], [bias]).T
            value_cols[:, there] = extended(kv[e][HD:, here], [one])[:VE]
    queries = extended(qt[...], [jnp.ones((1, n), f32)])
    acc[...] = jnp.zeros_like(acc)
    top[...] = jnp.full_like(top, -1e30)

    def step(i, carry):
        starts = [pl.multiple_of(meta[1 + i * unroll + u] * size, size) for u in range(unroll)]
        scores = [
            jnp.dot(key_rows[pl.ds(s, size), :], queries, preferred_element_type=f32)
            for s in starts
        ]
        old = top[...]
        new = old
        for s in scores:
            new = jnp.maximum(new, jnp.max(s, axis=0, keepdims=True))
        total = acc[...] * jnp.exp(old - new)
        for s, start in zip(scores, starts):
            probs = jnp.exp(s - new).astype(bf16)
            total = total + jnp.dot(
                value_cols[:, pl.ds(start, size)], probs, preferred_element_type=f32
            )
        acc[...] = total
        top[...] = new
        return carry

    lax.fori_loop(0, (meta[0] + unroll - 1) // unroll, step, 0)
    exp_total = acc[HD : HD + 1, :]
    out = (acc[:HD, :] / exp_total).astype(bf16)
    for j in range(ot.shape[0]):
        ot[j] = out[:, j * ot.shape[2] : (j + 1) * ot.shape[2]]
    lse[0] = top[...] + jnp.log(exp_total)


def backward_kernel(meta, qt, ot, dot_t, lse, *refs, size, pieces, inner):
    kv = refs[:pieces]
    dq, keep, send = refs[pieces : pieces + 3]
    key_cols, value_cols, key_rows, query_rows, grad_rows, grad_cols, dq_acc = refs[pieces + 3 :]
    blocks = pieces * inner
    half = keep.shape[0]
    n = qt.shape[1]
    one = jnp.ones((1, size), f32)
    for e in range(pieces):
        for j in range(inner):
            b = e * inner + j
            here = slice(j * size, (j + 1) * size)
            there = slice(b * size, (b + 1) * size)
            bias = key_bias(meta, b, size, blocks)
            keys = extended(kv[e][:HD, here], [bias, one, one, one])
            key_cols[:, there] = keys
            key_rows[there, :] = keys.T
            value_cols[:, there] = extended(kv[e][HD:, here], [one, one])
    minus = -lse[0]
    high = minus.astype(bf16).astype(f32)
    mid = (minus - high).astype(bf16).astype(f32)
    query_rows[...] = extended(qt[...], [jnp.ones((1, n), f32), high, mid, minus - high - mid]).T
    grads = jnp.concatenate([dot_t[j] for j in range(dot_t.shape[0])], 1)
    outs = jnp.concatenate([ot[j] for j in range(ot.shape[0])], 1)
    grad_cols[...] = grads
    row_dot = -jnp.sum(grads.astype(f32) * outs.astype(f32), axis=0, keepdims=True)
    high = row_dot.astype(bf16).astype(f32)
    grad_rows[...] = extended(grads, [high, row_dot - high]).T
    dq_acc[...] = jnp.zeros_like(dq_acc)
    keep[...] = jnp.zeros_like(keep)
    send[...] = jnp.zeros_like(send)

    def step(i, carry):
        b = meta[1 + i]
        start = pl.multiple_of(b * size, size)
        probs = jnp.exp(
            jnp.dot(query_rows[...], key_cols[:, pl.ds(start, size)], preferred_element_type=f32)
        )
        centred = jnp.dot(
            grad_rows[...], value_cols[:, pl.ds(start, size)], preferred_element_type=f32
        )
        score_grad = (probs * centred).astype(bf16)
        dq_acc[...] += jnp.dot(
            score_grad, key_rows[pl.ds(start, size), :], preferred_element_type=f32
        )
        dk = jnp.dot(qt[...], score_grad, preferred_element_type=f32).astype(bf16)
        dv = jnp.dot(grad_cols[...], probs.astype(bf16), preferred_element_type=f32).astype(bf16)
        lane = pl.multiple_of((b % inner) * size, size)
        piece = b // inner

        @pl.when(piece < half)
        def _():
            keep[piece, :HD, pl.ds(lane, size)] = dk
            keep[piece, HD:, pl.ds(lane, size)] = dv

        @pl.when(piece >= half)
        def _():
            send[piece - half, :HD, pl.ds(lane, size)] = dk
            send[piece - half, HD:, pl.ds(lane, size)] = dv

        return carry

    lax.fori_loop(0, meta[0], step, 0)
    dq[...] = (dq_acc[...].T[:HD] * HD ** (-0.5)).astype(bf16)


def attend_forward(meta, qt, kvs, size, first, count):
    n, pieces = qt.shape[1], len(kvs)
    columns = kvs[0].shape[1]
    inner = columns // size
    keys = pieces * columns
    unroll = 2 if (pieces * inner) % 2 == 0 else 1
    return pl.pallas_call(
        functools.partial(
            forward_kernel, size=size, pieces=pieces, inner=inner, unroll=unroll
        ),
        grid_spec=pltpu.PrefetchScalarGridSpec(
            num_scalar_prefetch=1,
            grid=(count,),
            in_specs=[pl.BlockSpec((HD, n), lambda h, m: (first + h, 0))]
            + [pl.BlockSpec((2 * HD, columns), lambda h, m: (first + h, 0))] * pieces,
            out_specs=[
                pl.BlockSpec((n // size, HD, size), lambda h, m: (0, h, 0)),
                pl.BlockSpec((1, 1, n), lambda h, m: (h, 0, 0)),
            ],
            scratch_shapes=[
                pltpu.VMEM((keys, EXT), bf16),
                pltpu.VMEM((VE, keys), bf16),
                pltpu.VMEM((VE, n), f32),
                pltpu.VMEM((1, n), f32),
            ],
        ),
        out_shape=[
            jax.ShapeDtypeStruct((n // size, count * HD, size), bf16),
            jax.ShapeDtypeStruct((count, 1, n), f32),
        ],
        cost_estimate=pl.CostEstimate(
            flops=20 * count * HD * n * keys,
            bytes_accessed=8 * count * HD * n,
            transcendentals=0,
        ),
        name="attend_forward",
    )(meta, qt, *kvs)


def attend_backward(meta, qt, ot, dot_t, lse, kvs, size, first, count, seq):
    n, pieces = qt.shape[1], len(kvs)
    columns = kvs[0].shape[1]
    inner = columns // size
    keys = pieces * columns
    half = (pieces + 1) // 2
    row_spec = pl.BlockSpec((HD, n), lambda h, m: (first + h, 0))
    split_spec = pl.BlockSpec((n // size, HD, size), lambda h, m: (0, first + h, 0))
    grad_spec = pl.BlockSpec((n // size, HD, size), lambda h, m: (0, first + h, seq))
    part_spec = pl.BlockSpec((half, 2 * HD, columns), lambda h, m: (0, h, 0))
    part_shape = jax.ShapeDtypeStruct((half, 2 * HD * count, columns), bf16)
    return pl.pallas_call(
        functools.partial(backward_kernel, size=size, pieces=pieces, inner=inner),
        grid_spec=pltpu.PrefetchScalarGridSpec(
            num_scalar_prefetch=1,
            grid=(count,),
            in_specs=[row_spec, split_spec, grad_spec]
            + [pl.BlockSpec((1, 1, n), lambda h, m: (first + h, 0, 0))]
            + [pl.BlockSpec((2 * HD, columns), lambda h, m: (first + h, 0))] * pieces,
            out_specs=[pl.BlockSpec((HD, n), lambda h, m: (h, 0)), part_spec, part_spec],
            scratch_shapes=[
                pltpu.VMEM((EXT, keys), bf16),
                pltpu.VMEM((EXT, keys), bf16),
                pltpu.VMEM((keys, EXT), bf16),
                pltpu.VMEM((n, EXT), bf16),
                pltpu.VMEM((n, EXT), bf16),
                pltpu.VMEM((HD, n), bf16),
                pltpu.VMEM((n, EXT), f32),
            ],
        ),
        out_shape=[jax.ShapeDtypeStruct((count * HD, n), bf16), part_shape, part_shape],
        cost_estimate=pl.CostEstimate(
            flops=count * HD * n,
            bytes_accessed=count * HD * n,
            transcendentals=0,
        ),
        name="attend_backward",
    )(meta, qt, ot, dot_t, lse, *kvs)


def pair_kernel(left_a, right_a, left_b, right_b, out):
    for place, left, right in ((0, left_a, right_a), (1, left_b, right_b)):

        @pl.when(pl.program_id(0) == place)
        def _():
            out[0] = lax.dot_general(
                left[...], right[...], (((0,), (0,)), ((), ())), preferred_element_type=f32
            ).astype(bf16)


def weight_grad_pair(left_a, right_a, left_b, right_b, tile):
    n, columns = left_a.shape
    tiles = columns // tile
    width = right_a.shape[1]
    whole = pl.BlockSpec((n, width), lambda g, i: (0, 0))
    return pl.pallas_call(
        pair_kernel,
        grid=(2, tiles),
        in_specs=[
            pl.BlockSpec((n, tile), lambda g, i: (0, i * (1 - g) + (tiles - 1) * g)),
            whole,
            pl.BlockSpec((n, tile), lambda g, i: (0, i * g)),
            whole,
        ],
        out_specs=pl.BlockSpec((1, tile, width), lambda g, i: (g, i, 0)),
        out_shape=jax.ShapeDtypeStruct((2, columns, width), bf16),
        cost_estimate=pl.CostEstimate(
            flops=4 * n * columns * width, bytes_accessed=8 * n * columns, transcendentals=0
        ),
        name="weight_grad_pair",
    )(left_a, right_a, left_b, right_b)


def swap(x, axis, bits):
    return lax.ppermute(x, axis, [(i, i ^ bits) for i in range(lax.axis_size(axis))])


def wide(x):
    return x.astype(f32)


def low(x):
    return x.astype(bf16)


def dot(a, b, contract):
    return lax.dot_general(a, b, (contract, ((), ())), preferred_element_type=f32)


NN = ((1,), (0,))
NT = ((1,), (1,))
TN = ((0,), (0,))


def xor_order(x, axis, index):
    n = x.shape[axis]
    bit = 1
    while bit < n:
        moved = jnp.stack([lax.index_in_dim(x, i ^ bit, axis, False) for i in range(n)], axis)
        x = jnp.where((index & bit) != 0, moved, x)
        bit *= 2
    return x


def norm_forward(resid, gain, shift):
    centre = resid - jnp.mean(resid, axis=-1, keepdims=True)
    factor = lax.rsqrt(jnp.mean(centre * centre, axis=-1, keepdims=True) + epsilon)
    normed = centre * factor
    return (normed * gain + shift, normed, factor)


def norm_backward(grad_out, normed, factor, gain):
    scaled = grad_out * gain
    centred = scaled - jnp.mean(scaled, axis=-1, keepdims=True)
    return factor * (centred - normed * jnp.mean(scaled * normed, axis=-1, keepdims=True))


def on_device(
    tokens,
    cotangent,
    lengths,
    query_weight,
    query_bias,
    key_weight,
    value_weight,
    value_bias,
    out_weight,
    out_bias,
    first_gain,
    first_shift,
    up_weight,
    up_bias,
    down_weight,
    down_bias,
    second_gain,
    second_shift,
):
    shard_n, ctx_n, tp_n = (lax.axis_size(a) for a in ("shard", "ctx", "tp"))
    shard_i, ctx_i, tp_i = (lax.axis_index(a) for a in ("shard", "ctx", "tp"))
    seqs, rows, model = tokens.shape
    part = model // shard_n
    width = query_weight.shape[1]
    heads = width // HD
    units = up_weight.shape[1]
    quarter = units // ctx_n
    two = shard_n == 2
    first = shard_i == 0

    def flip(x):
        if not two:
            return x
        return jnp.where(first, x, jnp.concatenate([x[..., part:], x[..., :part]], -1))

    def gather_local(x):
        if two:
            return jnp.concatenate([x, swap(x, "shard", 1)], -1)
        return lax.all_gather(x, "shard", axis=x.ndim - 1, tiled=True)

    def scatter_local(x):
        if two:
            return wide(x[:, :part]) + wide(swap(x[:, part:], "shard", 1))
        return wide(lax.psum_scatter(x, "shard", scatter_dimension=1, tiled=True))

    def after(x, *gates):
        return lax.optimization_barrier((x, *gates))[0]

    bits = ctx_n.bit_length() - 1
    ctx_bits = [1 << i for i in reversed(range(bits))]

    def bit_reverse(e):
        return sum(((e >> i) & 1) << (bits - 1 - i) for i in range(bits))

    ctx_order = [bit_reverse(e) for e in range(ctx_n)]
    half = (ctx_n + 1) // 2

    def exchange(x):
        return lax.all_to_all(x, "tp", 0, 0, tiled=True)

    def tp_gather(x):
        return exchange(jnp.broadcast_to(x[None], (tp_n, *x.shape)))

    def ctx_gather(chunks):
        for bit in ctx_bits:
            chunks = chunks + [swap(c, "ctx", bit) for c in chunks]
        return chunks

    kv_t = jnp.stack(
        [key_weight.T.reshape(heads, HD, part), value_weight.T.reshape(heads, HD, part)], 1
    ).reshape(2 * width, part)
    mine = lambda w: lax.dynamic_slice_in_dim(w, ctx_i * quarter, quarter, 0)
    weights = jnp.concatenate(
        [query_weight.T, kv_t, mine(up_weight.T), mine(down_weight), out_weight], 0
    )
    weights = flip(gather_local(weights))
    qkv_t = weights[: 3 * width]
    up_down = weights[3 * width : 3 * width + 2 * quarter].reshape(2, quarter, model)
    out_own = weights[3 * width + 2 * quarter :]

    first_in = tp_gather(tokens[0])
    bias_rows = []
    rest = up_bias
    for _ in range(3):
        bias_rows.append(low(rest))
        rest = rest - wide(bias_rows[-1])
    bias_rows = jnp.stack(bias_rows, 0)
    extra = units * 3 // model
    fill = -(width + extra) % 16
    out_own = jnp.concatenate(
        [out_own, bias_rows.reshape(extra, model), jnp.zeros((fill, model), bf16)], 0
    )
    blocks = [first_in.reshape(tp_n * rows, model)]
    for s in range(1, seqs):
        blocks.append(tp_gather(after(tokens[s], blocks[-1])).reshape(tp_n * rows, model))
    out_all = tp_gather(after(out_own, blocks[-1]))
    kv_bias = jnp.stack(
        [jnp.zeros((heads, HD), f32), value_bias.reshape(heads, HD)], 1
    ).reshape(2 * width, 1)
    up_down = lax.all_gather(after(up_down, first_in), ("ctx", "tp"), axis=1, tiled=True)
    up_full, down_full = up_down[0], up_down[1]
    out_full = out_all[:, :width].reshape(tp_n * width, model)
    unit_bias = wide(out_all[:, width : width + extra]).reshape(tp_n, 3, ctx_n, quarter)
    unit_bias = (unit_bias[:, 0] + unit_bias[:, 1]) + unit_bias[:, 2]
    unit_bias = unit_bias.transpose(1, 0, 2).reshape(1, ctx_n * tp_n * quarter)

    place = jnp.arange(ctx_n * tp_n)
    order = bit_reverse((place // tp_n) ^ ctx_i) * tp_n + place % tp_n
    block_at = (bit_reverse(place // tp_n) ^ ctx_i) * tp_n + place % tp_n

    def project(s, block):
        kv = low(dot(qkv_t[width:], block, NT) + kv_bias)
        q = low(dot(qkv_t[:width], block, NT) + query_bias[:, None])
        return kv, q * bf16(HD ** (-0.5))

    def ctx_pieces(kv, gate):
        chunks = [kv]
        for bit in ctx_bits:
            chunks = chunks + [swap(c, "ctx", bit) for c in chunks]
            if gate is not None and bit == ctx_bits[0]:
                chunks = [after(c, gate) for c in chunks]
        return chunks

    metas = []
    for s in range(seqs):
        count = jnp.clip(lengths[s] - block_at * rows, 0, rows)
        metas.append(
            jnp.concatenate([((lengths[s] + rows - 1) // rows)[None], order, count]).astype(
                jnp.int32
            )
        )

    outs, totals, attended, queries, keys_values = [], [], [], [], []
    kv, q = project(0, blocks[0])
    kvs = ctx_pieces(kv, None)
    for s in range(seqs):
        keys_values.append(kvs)
        queries.append(q)
        if s + 1 < seqs and heads > 1:
            ot_a, lse_a = attend_forward(metas[s], q, kvs, rows, 0, heads - 1)
            kv_next, q_next = project(s + 1, after(blocks[s + 1], lse_a))
            meta = after(metas[s], kv_next, q_next)
            ot_b, lse_b = attend_forward(meta, q, kvs, rows, heads - 1, 1)
            ot = jnp.concatenate([ot_a, ot_b], 1)
            lse = jnp.concatenate([lse_a, lse_b], 0)
            q, kvs = q_next, ctx_pieces(kv_next, lse_b)
            ot = after(ot, out_all)
        else:
            ot, lse = attend_forward(metas[s], q, kvs, rows, 0, heads)
        outs.append(ot)
        totals.append(lse)
        attended.append(exchange(ot).reshape(tp_n * width, rows))
    attended_t = jnp.concatenate(attended, 1)

    flat = wide(tokens.reshape(seqs * rows, model))
    cot = wide(cotangent.reshape(seqs * rows, model))
    mixed = dot(attended_t, out_full, TN) + out_bias
    hidden, normed_1, factor_1 = norm_forward(flat + mixed, first_gain, first_shift)
    hidden_low = low(hidden)
    pre = dot(hidden_low, up_full, NT) + unit_bias
    share = 0.5 * (1.0 + lax.erf(pre * 0.5**0.5))
    activated = low(pre * share)
    slope = low(share + pre * jnp.exp(-0.5 * pre * pre) * 0.3989422804014327)
    ffn_out = dot(activated, down_full, NN) + down_bias
    result, normed_2, factor_2 = norm_forward(hidden + ffn_out, second_gain, second_shift)
    here = (ctx_i * tp_n + tp_i) * rows + jnp.arange(rows)
    valid = (here[None, :] < lengths[:, None]).reshape(seqs * rows, 1)
    grad_result = jnp.where(valid, cot, 0.0)
    gain_2_grad = jnp.sum(grad_result * normed_2, axis=0)
    shift_2_grad = jnp.sum(grad_result, axis=0)
    grad_second = norm_backward(grad_result, normed_2, factor_2, second_gain)
    ffn_grad = low(grad_second)
    bias_d_grad = jnp.sum(wide(ffn_grad), axis=0)
    pre_grad = low(dot(ffn_grad, down_full, NT) * wide(slope))
    grad_hidden = grad_second + dot(pre_grad, up_full, NN)
    up_bias_grad = jnp.sum(wide(pre_grad), axis=0)
    gain_1_grad = jnp.sum(grad_hidden * normed_1, axis=0)
    shift_1_grad = jnp.sum(grad_hidden, axis=0)
    grad_first = norm_backward(grad_hidden, normed_1, factor_1, first_gain)
    mixer_grad = low(grad_first)
    bias_o_grad = jnp.sum(wide(mixer_grad), axis=0)
    attended_grad_t = low(dot(out_full, mixer_grad, NT))
    value_bias_parts = jnp.sum(
        wide(attended_grad_t).reshape(tp_n, width, seqs * rows), axis=2
    )
    value_bias_grad = value_bias_parts.reshape(-1)
    up_bias_full = up_bias_grad.reshape(ctx_n, tp_n, quarter).transpose(1, 0, 2).reshape(-1)
    vectors = [
        value_bias_grad,
        bias_o_grad,
        gain_1_grad,
        shift_1_grad,
        up_bias_full,
        bias_d_grad,
        gain_2_grad,
        shift_2_grad,
    ]
    sizes = [v.shape[0] for v in vectors]
    summed = 0.0
    for i, v in enumerate(vectors):
        summed = summed + jnp.pad(v, (sum(sizes[:i]), sum(sizes[i + 1 :])))

    def all_sum(x, axis):
        n = lax.axis_size(axis)
        if n & (n - 1):
            return lax.psum(x, axis)
        for i in range(n.bit_length() - 1):
            x = x + swap(x, axis, 1 << i)
        return x


    grad_cols = exchange(attended_grad_t.reshape(tp_n, width, seqs * rows))

    def sum_ctx(x):
        for bit in reversed(ctx_bits):
            x = low(x)
            x = wide(x) + wide(swap(x, "ctx", bit))
        return x

    late_pre = after(pre_grad, attended_grad_t)
    ffn_grads = weight_grad_pair(late_pre, hidden_low, activated, ffn_grad, quarter * ctx_n)
    ffn_sum = lax.psum_scatter(ffn_grads, ("ctx", "tp"), scatter_dimension=1, tiled=True)
    out_grad = low(dot(attended_t, mixer_grad, NN))

    grad_rows = grad_first.reshape(seqs, rows, model)
    spans = []
    for s in range(seqs):
        if s + 1 < seqs or heads == 1:
            spans.append((s, 0, heads))
        else:
            spans += [(s, 0, heads - 1), (s, heads - 1, 1)]
    near = ctx_bits[-1:]
    far = list(reversed(ctx_bits[:-1]))

    def near_sum(keep, send):
        total = wide(keep)
        for bit in near:
            total = total + wide(swap(send, "ctx", bit))
        return [low(total[p]) for p in range(half)]

    def far_sum(chunks):
        for bit in far:
            n = len(chunks) // 2
            chunks = [
                low(wide(a) + wide(swap(b, "ctx", bit))) for a, b in zip(chunks[:n], chunks[n:])
            ]
        return chunks[0]

    def tp_sum(x):
        x = exchange(x.reshape(tp_n, x.shape[0] // tp_n, x.shape[1]))
        return jnp.sum(wide(x), axis=0)

    qkv_grad = 0.0
    sums = 0.0
    input_parts = []
    dq_parts = [[] for _ in range(seqs)]
    dkv_parts = [[] for _ in range(seqs)]
    last = ()
    near_chunks = None
    number = 0

    def finish(s):
        grads_t = jnp.concatenate(dq_parts[s] + dkv_parts[s], 0)
        back = low(dot(grads_t, qkv_t, TN))
        return (
            back,
            low(
                grad_rows[s]
                + wide(lax.psum_scatter(back, "tp", scatter_dimension=0, tiled=True))
            ),
            dot(grads_t, blocks[s], NN),
            jnp.sum(wide(jnp.concatenate(dq_parts[s], 0)), axis=1),
        )

    def take(done):
        return (input_parts + [done[1]], qkv_grad + done[2], sums + done[3])

    for s, start, count in spans:
        meta = metas[s]
        wait = list(last) if last else [grad_cols]
        if number >= 1:
            wait += near_chunks
        if number == 1:
            out_grad = low(scatter_local(flip(out_grad)))
            wait += [out_grad]
        if number >= 2:
            done_s = spans[number - 2][0]
            wait.append(dkv_parts[done_s][-1])
            if spans[number - 1][0] != done_s:
                done = finish(done_s)
                wait.append(done[0])
                input_parts, qkv_grad, sums = take(done)
            if number == 2:
                out_grad = tp_sum(out_grad)
                summed = all_sum(summed, "tp")
                wait += [out_grad, summed]
        if wait:
            meta = after(meta, *wait)
        dq, keep, send = attend_backward(
            meta, queries[s], outs[s], grad_cols, totals[s], keys_values[s], rows, start, count, s
        )
        last = (dq,)
        number += 1
        near_chunks = near_sum(keep, send)
        dq_parts[s].append(dq)
        dkv_parts[s].append(far_sum(near_chunks))
    if number == 1:
        out_grad = low(scatter_local(flip(out_grad)))
    if number <= 2:
        out_grad = tp_sum(out_grad)
        summed = all_sum(summed, "tp")
    summed = all_sum(all_sum(summed, "ctx"), "shard")
    input_parts, qkv_grad, sums = take(finish(seqs - 1))
    input_grads = jnp.stack(input_parts, 0)
    out_sum = sum_ctx(out_grad)

    ffn_sum = scatter_local(flip(ffn_sum.reshape(2 * quarter, model)))
    chunks = ctx_gather([low(ffn_sum)])
    stacked = jnp.stack([chunks[ctx_order.index(e)] for e in range(ctx_n)], 0)
    stacked = wide(xor_order(stacked, 0, ctx_i))
    up_sum = stacked[:, :quarter].reshape(units, part)
    down_sum = stacked[:, quarter:].reshape(units, part)

    qkv_sum = sum_ctx(scatter_local(flip(low(qkv_grad))))
    query_sum = qkv_sum[:width]
    kv_sum = qkv_sum[width:].reshape(heads, 2, HD, part)
    key_sum = kv_sum[:, 0].reshape(width, part)
    value_sum = kv_sum[:, 1].reshape(width, part)

    query_bias_sum = all_sum(all_sum(sums, "ctx"), "shard")
    query_bias_full = tp_gather(query_bias_sum).reshape(-1)
    ends = []
    at = 0
    for n in sizes:
        ends.append(summed[at : at + n])
        at += n
    return (
        low(result).reshape(seqs, rows, model),
        input_grads,
        query_sum.T,
        query_bias_full,
        key_sum.T,
        value_sum.T,
        ends[0],
        out_sum,
        ends[1],
        ends[2],
        ends[3],
        up_sum.T,
        ends[4],
        down_sum,
        ends[5],
        ends[6],
        ends[7],
    )


def solution(mesh):
    placed = (
        P("shard", ("ctx", "tp"), None),
        P("shard", ("ctx", "tp"), None),
        P("shard"),
        P("shard", "tp"),
        P("tp"),
        P("shard", "tp"),
        P("shard", "tp"),
        P("tp"),
        P("tp", "shard"),
        P(),
        P(),
        P(),
        P("shard", "tp"),
        P("tp"),
        P("tp", "shard"),
        P(),
        P(),
        P(),
    )
    return jax.shard_map(
        on_device,
        mesh=mesh,
        in_specs=placed,
        out_specs=(
            P("shard", ("ctx", "tp"), None),
            P("shard", ("ctx", "tp"), None),
            P("shard", "tp"),
            P(),
            P("shard", "tp"),
            P("shard", "tp"),
            P(),
            P("tp", "shard"),
            P(),
            P(),
            P(),
            P("shard", "tp"),
            P(),
            P("tp", "shard"),
            P(),
            P(),
            P(),
        ),
        check_vma=False,
    )
```

```python
import functools

import jax
import jax.numpy as jnp
from jax import lax
from jax.experimental import pallas as pl
from jax.experimental.pallas import tpu as pltpu
from jax.sharding import PartitionSpec as P

HD = 64
EXT = 128
VE = 80
epsilon = 1e-12
f32 = jnp.float32
bf16 = jnp.bfloat16


def extended(block, extra_rows):
    n = block.shape[1]
    row = lax.broadcasted_iota(jnp.int32, (EXT - HD, n), 0)
    extra = jnp.zeros((EXT - HD, n), f32)
    for place, values in enumerate(extra_rows):
        extra = jnp.where(row == place, values, extra)
    return jnp.concatenate([block, extra.astype(bf16)], axis=0)


def key_bias(meta, block, size, blocks):
    count = meta[1 + blocks + block]
    lane = lax.broadcasted_iota(jnp.int32, (1, size), 1)
    return jnp.where(lane < count, 0.0, -1e30).astype(f32)


def forward_kernel(meta, qt, *refs, size, pieces, inner, unroll):
    kv = refs[:pieces]
    ot, lse, key_rows, value_cols, acc, top = refs[pieces:]
    blocks = pieces * inner
    n = qt.shape[1]
    one = jnp.ones((1, size), f32)
    for e in range(pieces):
        for j in range(inner):
            b = e * inner + j
            here = slice(j * size, (j + 1) * size)
            there = slice(b * size, (b + 1) * size)
            bias = key_bias(meta, b, size, blocks)
            key_rows[there, :] = extended(kv[e][:HD, here], [bias]).T
            value_cols[:, there] = extended(kv[e][HD:, here], [one])[:VE]
    queries = extended(qt[...], [jnp.ones((1, n), f32)])
    acc[...] = jnp.zeros_like(acc)
    top[...] = jnp.full_like(top, -1e30)

    def step(i, carry):
        starts = [pl.multiple_of(meta[1 + i * unroll + u] * size, size) for u in range(unroll)]
        scores = [
            jnp.dot(key_rows[pl.ds(s, size), :], queries, preferred_element_type=f32)
            for s in starts
        ]
        old = top[...]
        new = old
        for s in scores:
            new = jnp.maximum(new, jnp.max(s, axis=0, keepdims=True))
        total = acc[...] * jnp.exp(old - new)
        for s, start in zip(scores, starts):
            probs = jnp.exp(s - new).astype(bf16)
            total = total + jnp.dot(
                value_cols[:, pl.ds(start, size)], probs, preferred_element_type=f32
            )
        acc[...] = total
        top[...] = new
        return carry

    lax.fori_loop(0, (meta[0] + unroll - 1) // unroll, step, 0)
    exp_total = acc[HD : HD + 1, :]
    out = (acc[:HD, :] / exp_total).astype(bf16)
    for j in range(ot.shape[0]):
        ot[j] = out[:, j * ot.shape[2] : (j + 1) * ot.shape[2]]
    lse[0] = top[...] + jnp.log(exp_total)


def backward_kernel(meta, qt, ot, dot_t, lse, *refs, size, pieces, inner):
    kv = refs[:pieces]
    dq, keep, send = refs[pieces : pieces + 3]
    key_cols, value_cols, key_rows, query_rows, grad_rows, grad_cols, dq_acc = refs[pieces + 3 :]
    blocks = pieces * inner
    half = keep.shape[0]
    n = qt.shape[1]
    one = jnp.ones((1, size), f32)
    for e in range(pieces):
        for j in range(inner):
            b = e * inner + j
            here = slice(j * size, (j + 1) * size)
            there = slice(b * size, (b + 1) * size)
            bias = key_bias(meta, b, size, blocks)
            keys = extended(kv[e][:HD, here], [bias, one, one, one])
            key_cols[:, there] = keys
            key_rows[there, :] = keys.T
            value_cols[:, there] = extended(kv[e][HD:, here], [one, one])
    minus = -lse[0]
    high = minus.astype(bf16).astype(f32)
    mid = (minus - high).astype(bf16).astype(f32)
    query_rows[...] = extended(qt[...], [jnp.ones((1, n), f32), high, mid, minus - high - mid]).T
    grads = jnp.concatenate([dot_t[j] for j in range(dot_t.shape[0])], 1)
    outs = jnp.concatenate([ot[j] for j in range(ot.shape[0])], 1)
    grad_cols[...] = grads
    row_dot = -jnp.sum(grads.astype(f32) * outs.astype(f32), axis=0, keepdims=True)
    high = row_dot.astype(bf16).astype(f32)
    grad_rows[...] = extended(grads, [high, row_dot - high]).T
    dq_acc[...] = jnp.zeros_like(dq_acc)
    keep[...] = jnp.zeros_like(keep)
    send[...] = jnp.zeros_like(send)

    def step(i, carry):
        b = meta[1 + i]
        start = pl.multiple_of(b * size, size)
        probs = jnp.exp(
            jnp.dot(query_rows[...], key_cols[:, pl.ds(start, size)], preferred_element_type=f32)
        )
        centred = jnp.dot(
            grad_rows[...], value_cols[:, pl.ds(start, size)], preferred_element_type=f32
        )
        score_grad = (probs * centred).astype(bf16)
        dq_acc[...] += jnp.dot(
            score_grad, key_rows[pl.ds(start, size), :], preferred_element_type=f32
        )
        dk = jnp.dot(qt[...], score_grad, preferred_element_type=f32).astype(bf16)
        dv = jnp.dot(grad_cols[...], probs.astype(bf16), preferred_element_type=f32).astype(bf16)
        lane = pl.multiple_of((b % inner) * size, size)
        piece = b // inner

        @pl.when(piece < half)
        def _():
            keep[piece, :HD, pl.ds(lane, size)] = dk
            keep[piece, HD:, pl.ds(lane, size)] = dv

        @pl.when(piece >= half)
        def _():
            send[piece - half, :HD, pl.ds(lane, size)] = dk
            send[piece - half, HD:, pl.ds(lane, size)] = dv

        return carry

    lax.fori_loop(0, meta[0], step, 0)
    dq[...] = (dq_acc[...].T[:HD] * HD ** (-0.5)).astype(bf16)


def attend_forward(meta, qt, kvs, size, first, count):
    n, pieces = qt.shape[1], len(kvs)
    columns = kvs[0].shape[1]
    inner = columns // size
    keys = pieces * columns
    unroll = 2 if (pieces * inner) % 2 == 0 else 1
    return pl.pallas_call(
        functools.partial(
            forward_kernel, size=size, pieces=pieces, inner=inner, unroll=unroll
        ),
        grid_spec=pltpu.PrefetchScalarGridSpec(
            num_scalar_prefetch=1,
            grid=(count,),
            in_specs=[pl.BlockSpec((HD, n), lambda h, m: (first + h, 0))]
            + [pl.BlockSpec((2 * HD, columns), lambda h, m: (first + h, 0))] * pieces,
            out_specs=[
                pl.BlockSpec((n // size, HD, size), lambda h, m: (0, h, 0)),
                pl.BlockSpec((1, 1, n), lambda h, m: (h, 0, 0)),
            ],
            scratch_shapes=[
                pltpu.VMEM((keys, EXT), bf16),
                pltpu.VMEM((VE, keys), bf16),
                pltpu.VMEM((VE, n), f32),
                pltpu.VMEM((1, n), f32),
            ],
        ),
        out_shape=[
            jax.ShapeDtypeStruct((n // size, count * HD, size), bf16),
            jax.ShapeDtypeStruct((count, 1, n), f32),
        ],
        cost_estimate=pl.CostEstimate(
            flops=20 * count * HD * n * keys,
            bytes_accessed=8 * count * HD * n,
            transcendentals=0,
        ),
        name="attend_forward",
    )(meta, qt, *kvs)


def attend_backward(meta, qt, ot, dot_t, lse, kvs, size, first, count, seq):
    n, pieces = qt.shape[1], len(kvs)
    columns = kvs[0].shape[1]
    inner = columns // size
    keys = pieces * columns
    half = (pieces + 1) // 2
    row_spec = pl.BlockSpec((HD, n), lambda h, m: (first + h, 0))
    split_spec = pl.BlockSpec((n // size, HD, size), lambda h, m: (0, first + h, 0))
    grad_spec = pl.BlockSpec((n // size, HD, size), lambda h, m: (0, first + h, seq))
    part_spec = pl.BlockSpec((half, 2 * HD, columns), lambda h, m: (0, h, 0))
    part_shape = jax.ShapeDtypeStruct((half, 2 * HD * count, columns), bf16)
    return pl.pallas_call(
        functools.partial(backward_kernel, size=size, pieces=pieces, inner=inner),
        grid_spec=pltpu.PrefetchScalarGridSpec(
            num_scalar_prefetch=1,
            grid=(count,),
            in_specs=[row_spec, split_spec, grad_spec]
            + [pl.BlockSpec((1, 1, n), lambda h, m: (first + h, 0, 0))]
            + [pl.BlockSpec((2 * HD, columns), lambda h, m: (first + h, 0))] * pieces,
            out_specs=[pl.BlockSpec((HD, n), lambda h, m: (h, 0)), part_spec, part_spec],
            scratch_shapes=[
                pltpu.VMEM((EXT, keys), bf16),
                pltpu.VMEM((EXT, keys), bf16),
                pltpu.VMEM((keys, EXT), bf16),
                pltpu.VMEM((n, EXT), bf16),
                pltpu.VMEM((n, EXT), bf16),
                pltpu.VMEM((HD, n), bf16),
                pltpu.VMEM((n, EXT), f32),
            ],
        ),
        out_shape=[jax.ShapeDtypeStruct((count * HD, n), bf16), part_shape, part_shape],
        cost_estimate=pl.CostEstimate(
            flops=count * HD * n,
            bytes_accessed=count * HD * n,
            transcendentals=0,
        ),
        name="attend_backward",
    )(meta, qt, ot, dot_t, lse, *kvs)


def weight_grad_kernel(
    pre, hidden, act, grad, mixed_t, mixer, vectors, out, mixed_sum, *, tp_n, step, tail
):
    half, piece = pl.program_id(0), pl.program_id(1)

    @pl.when((half == 0) & (piece == 0))
    def _():
        mixed_sum[...] = jnp.dot(mixed_t[...], mixer[...], preferred_element_type=f32)

    quarter = pre.shape[1] // tp_n

    def fill(left, right):
        found = lax.dot_general(
            left, right, (((0,), (0,)), ((), ())), preferred_element_type=f32
        ).astype(bf16)
        for t in range(tp_n):
            out[0, t * step : t * step + quarter, :] = found[t * quarter : (t + 1) * quarter]

    @pl.when(half == 0)
    def _():
        fill(pre[...], hidden[...])

    @pl.when(half == 1)
    def _():
        fill(act[...], grad[...])

    width = mixed_sum.shape[0] // tp_n
    for t in range(tp_n):
        start = pl.multiple_of(t * width + (piece * 2 + half) * tail, 8)
        ending = jnp.concatenate([mixed_sum[pl.ds(start, tail), :], vectors[half]], 0)
        out[0, t * step + quarter : (t + 1) * step, :] = ending.astype(bf16)


def weight_grads(pre, hidden, act, grad, mixed_t, mixer, vectors, pieces, tp_n, step, tail):
    n, columns = pre.shape
    width = hidden.shape[1]
    tile = columns // pieces
    whole = lambda x: pl.BlockSpec(x.shape, lambda g, i: (0, 0))
    return pl.pallas_call(
        functools.partial(weight_grad_kernel, tp_n=tp_n, step=step, tail=tail),
        grid=(2, pieces),
        in_specs=[
            pl.BlockSpec((n, tile), lambda g, i: (0, i * (1 - g) + (pieces - 1) * g)),
            whole(hidden),
            pl.BlockSpec((n, tile), lambda g, i: (0, i * g)),
            whole(grad),
            whole(mixed_t),
            whole(mixer),
            pl.BlockSpec(vectors.shape, lambda g, i: (0, 0, 0)),
        ],
        out_specs=pl.BlockSpec((1, tp_n * step, width), lambda g, i: (g, i, 0)),
        out_shape=jax.ShapeDtypeStruct((2, pieces * tp_n * step, width), bf16),
        scratch_shapes=[pltpu.VMEM((mixed_t.shape[0], width), f32)],
        cost_estimate=pl.CostEstimate(
            flops=4 * n * columns * width, bytes_accessed=8 * n * columns, transcendentals=0
        ),
        name="weight_grads",
    )(pre, hidden, act, grad, mixed_t, mixer, vectors)


def swap(x, axis, bits):
    return lax.ppermute(x, axis, [(i, i ^ bits) for i in range(lax.axis_size(axis))])


def wide(x):
    return x.astype(f32)


def low(x):
    return x.astype(bf16)


def dot(a, b, contract):
    return lax.dot_general(a, b, (contract, ((), ())), preferred_element_type=f32)


NN = ((1,), (0,))
NT = ((1,), (1,))
TN = ((0,), (0,))


def xor_order(x, axis, index):
    n = x.shape[axis]
    bit = 1
    while bit < n:
        moved = jnp.stack([lax.index_in_dim(x, i ^ bit, axis, False) for i in range(n)], axis)
        x = jnp.where((index & bit) != 0, moved, x)
        bit *= 2
    return x


def norm_forward(resid, gain, shift):
    centre = resid - jnp.mean(resid, axis=-1, keepdims=True)
    factor = lax.rsqrt(jnp.mean(centre * centre, axis=-1, keepdims=True) + epsilon)
    normed = centre * factor
    return (normed * gain + shift, normed, factor)


def norm_backward(grad_out, normed, factor, gain):
    scaled = grad_out * gain
    centred = scaled - jnp.mean(scaled, axis=-1, keepdims=True)
    return factor * (centred - normed * jnp.mean(scaled * normed, axis=-1, keepdims=True))


def on_device(
    tokens,
    cotangent,
    lengths,
    query_weight,
    query_bias,
    key_weight,
    value_weight,
    value_bias,
    out_weight,
    out_bias,
    first_gain,
    first_shift,
    up_weight,
    up_bias,
    down_weight,
    down_bias,
    second_gain,
    second_shift,
):
    shard_n, ctx_n, tp_n = (lax.axis_size(a) for a in ("shard", "ctx", "tp"))
    shard_i, ctx_i, tp_i = (lax.axis_index(a) for a in ("shard", "ctx", "tp"))
    seqs, rows, model = tokens.shape
    part = model // shard_n
    width = query_weight.shape[1]
    heads = width // HD
    units = up_weight.shape[1]
    quarter = units // ctx_n
    two = shard_n == 2
    first = shard_i == 0

    def flip(x):
        if not two:
            return x
        return jnp.where(first, x, jnp.concatenate([x[..., part:], x[..., :part]], -1))

    def gather_local(x):
        if two:
            return jnp.concatenate([x, swap(x, "shard", 1)], -1)
        return lax.all_gather(x, "shard", axis=x.ndim - 1, tiled=True)

    def scatter_local(x):
        if two:
            return wide(x[:, :part]) + wide(swap(x[:, part:], "shard", 1))
        return wide(lax.psum_scatter(x, "shard", scatter_dimension=1, tiled=True))

    def after(x, *gates):
        return lax.optimization_barrier((x, *gates))[0]

    bits = ctx_n.bit_length() - 1
    ctx_bits = [1 << i for i in reversed(range(bits))]

    def bit_reverse(e):
        return sum(((e >> i) & 1) << (bits - 1 - i) for i in range(bits))

    ctx_order = [bit_reverse(e) for e in range(ctx_n)]
    half = (ctx_n + 1) // 2

    def exchange(x):
        return lax.all_to_all(x, "tp", 0, 0, tiled=True)

    def tp_gather(x):
        return exchange(jnp.broadcast_to(x[None], (tp_n, *x.shape)))

    def ctx_gather(chunks, some=None):
        for bit in ctx_bits if some is None else some:
            chunks = chunks + [swap(c, "ctx", bit) for c in chunks]
        return chunks

    kv_t = jnp.stack(
        [key_weight.T.reshape(heads, HD, part), value_weight.T.reshape(heads, HD, part)], 1
    ).reshape(2 * width, part)
    mine = lambda w: lax.dynamic_slice_in_dim(w, ctx_i * quarter, quarter, 0)
    qkv_t = flip(gather_local(jnp.concatenate([query_weight.T, kv_t], 0)))
    kv_bias = jnp.stack(
        [jnp.zeros((heads, HD), f32), value_bias.reshape(heads, HD)], 1
    ).reshape(2 * width, 1)

    first_in = tp_gather(tokens[0])
    blocks = [first_in.reshape(tp_n * rows, model)]
    for s in range(1, seqs):
        blocks.append(tp_gather(after(tokens[s], blocks[-1])).reshape(tp_n * rows, model))

    bias_rows = []
    rest = up_bias
    for _ in range(3):
        bias_rows.append(low(rest))
        rest = rest - wide(bias_rows[-1])
    extra = 3 * units // model
    bias_rows = jnp.stack(bias_rows, 0).reshape(extra, model)
    bias_rows = lax.dynamic_slice_in_dim(bias_rows, shard_i * part, part, 1)
    tail = width // ctx_n // 2
    step = -(-(quarter + tail + extra) // 16) * 16
    out_mine = lax.dynamic_slice_in_dim(out_weight, ctx_i * 2 * tail, 2 * tail, 0)
    fill = jnp.zeros((step - quarter - tail - extra, part), bf16)
    pack = jnp.stack(
        [
            jnp.concatenate([mine(up_weight.T), bias_rows, fill, out_mine[:tail]], 0),
            jnp.concatenate(
                [mine(down_weight), jnp.zeros((extra, part), bf16), fill, out_mine[tail:]], 0
            ),
        ],
        0,
    )
    pack = lax.all_gather(after(pack, blocks[-1]), "tp", axis=1, tiled=True)
    chunk = tp_n * step
    ups = [gather_local(pack[0])]
    downs = after(jnp.concatenate(ctx_gather([pack[1]], ctx_bits[:-1]), 0), *ups)

    place = jnp.arange(ctx_n * tp_n)
    order = bit_reverse((place // tp_n) ^ ctx_i) * tp_n + place % tp_n
    block_at = (bit_reverse(place // tp_n) ^ ctx_i) * tp_n + place % tp_n

    def project(s, block):
        kv = low(dot(qkv_t[width:], block, NT) + kv_bias)
        q = low(dot(qkv_t[:width], block, NT) + query_bias[:, None])
        return kv, q * bf16(HD ** (-0.5))

    def ctx_pieces(kv, gate):
        chunks = [kv]
        for bit in ctx_bits:
            chunks = chunks + [swap(c, "ctx", bit) for c in chunks]
            if gate is not None and bit == ctx_bits[0]:
                chunks = [after(c, gate) for c in chunks]
        return chunks

    metas = []
    for s in range(seqs):
        count = jnp.clip(lengths[s] - block_at * rows, 0, rows)
        metas.append(
            jnp.concatenate([((lengths[s] + rows - 1) // rows)[None], order, count]).astype(
                jnp.int32
            )
        )

    outs, totals, attended, queries, keys_values = [], [], [], [], []
    kv, q = project(0, blocks[0])
    kvs = ctx_pieces(kv, None)
    for s in range(seqs):
        keys_values.append(kvs)
        queries.append(q)
        if s + 1 < seqs and heads > 1:
            ot_a, lse_a = attend_forward(metas[s], q, kvs, rows, 0, heads - 1)
            kv_next, q_next = project(s + 1, after(blocks[s + 1], lse_a))
            meta = after(metas[s], kv_next, q_next)
            ot_b, lse_b = attend_forward(meta, q, kvs, rows, heads - 1, 1)
            ot = jnp.concatenate([ot_a, ot_b], 1)
            lse = jnp.concatenate([lse_a, lse_b], 0)
            q, kvs = q_next, ctx_pieces(kv_next, lse_b)
        else:
            ot_a, lse_a = attend_forward(metas[s], q, kvs, rows, 0, heads - 1)
            meta = after(metas[s], lse_a, ups[0], downs)
            ot_b, lse_b = attend_forward(meta, q, kvs, rows, heads - 1, 1)
            ot = jnp.concatenate([ot_a, ot_b], 1)
            lse = jnp.concatenate([lse_a, lse_b], 0)
        outs.append(ot)
        totals.append(lse)
        attended.append(exchange(ot).reshape(tp_n * width, rows))
    ups = ctx_gather(ups)
    downs = after(gather_local(downs), attended[-1])
    downs = [downs[i * chunk : (i + 1) * chunk] for i in range(half)]
    downs = ctx_gather(downs, ctx_bits[-1:])

    def natural(pieces):
        whole = jnp.zeros((ctx_n, *pieces[0].shape), bf16)
        for e, piece in zip(ctx_order, pieces):
            whole = lax.dynamic_update_slice_in_dim(whole, piece[None], e ^ ctx_i, 0)
        return whole

    ups = [x.reshape(tp_n, step, model) for x in ups]
    downs = [x.reshape(tp_n, step, model) for x in downs]
    up_full = natural([x[:, :quarter] for x in ups]).reshape(-1, model)
    down_full = natural([x[:, :quarter] for x in downs]).reshape(-1, model)
    ends = [
        jnp.stack([x[:, step - tail :] for x in pair], 1) for pair in zip(ups, downs)
    ]
    out_full = natural(ends).transpose(1, 0, 2, 3, 4).reshape(tp_n * width, model)
    unit_bias = wide(flip(ups[0][:, quarter : quarter + extra]))
    unit_bias = unit_bias.reshape(tp_n, 3, ctx_n, quarter)
    unit_bias = (unit_bias[:, 0] + unit_bias[:, 1]) + unit_bias[:, 2]
    unit_bias = unit_bias.transpose(1, 0, 2).reshape(1, ctx_n * tp_n * quarter)

    attended_t = jnp.concatenate(attended, 1)

    flat = flip(wide(tokens.reshape(seqs * rows, model)))
    cot = flip(wide(cotangent.reshape(seqs * rows, model)))
    gain_1, shift_1, gain_2, shift_2, bias_o, bias_d = (
        flip(v) for v in (first_gain, first_shift, second_gain, second_shift, out_bias, down_bias)
    )
    mixed = dot(attended_t, out_full, TN) + bias_o
    hidden, normed_1, factor_1 = norm_forward(flat + mixed, gain_1, shift_1)
    hidden_low = low(hidden)
    pre = dot(hidden_low, up_full, NT) + unit_bias
    share = 0.5 * (1.0 + lax.erf(pre * 0.5**0.5))
    activated = low(pre * share)
    slope = low(share + pre * jnp.exp(-0.5 * pre * pre) * 0.3989422804014327)
    ffn_out = dot(activated, down_full, NN) + bias_d
    result, normed_2, factor_2 = norm_forward(hidden + ffn_out, gain_2, shift_2)
    here = (ctx_i * tp_n + tp_i) * rows + jnp.arange(rows)
    valid = (here[None, :] < lengths[:, None]).reshape(seqs * rows, 1)
    grad_result = jnp.where(valid, cot, 0.0)
    gain_2_grad = jnp.sum(grad_result * normed_2, axis=0)
    shift_2_grad = jnp.sum(grad_result, axis=0)
    grad_second = norm_backward(grad_result, normed_2, factor_2, gain_2)
    ffn_grad = low(grad_second)
    bias_d_grad = jnp.sum(wide(ffn_grad), axis=0)
    pre_grad = low(dot(ffn_grad, down_full, NT) * wide(slope))
    grad_hidden = grad_second + dot(pre_grad, up_full, NN)
    up_bias_grad = jnp.sum(wide(pre_grad), axis=0)
    gain_1_grad = jnp.sum(grad_hidden * normed_1, axis=0)
    shift_1_grad = jnp.sum(grad_hidden, axis=0)
    grad_first = norm_backward(grad_hidden, normed_1, factor_1, gain_1)
    mixer_grad = low(grad_first)
    bias_o_grad = jnp.sum(wide(mixer_grad), axis=0)
    attended_grad_t = low(dot(out_full, mixer_grad, NT))
    value_bias_parts = jnp.sum(
        wide(attended_grad_t).reshape(tp_n, width, seqs * rows), axis=2
    )
    value_bias_grad = value_bias_parts.reshape(-1)
    up_bias_full = up_bias_grad.reshape(ctx_n, tp_n, quarter).transpose(1, 0, 2).reshape(-1)
    up_rows = up_bias_full.shape[0] // model
    vectors = [
        flip(value_bias_grad),
        bias_o_grad,
        gain_1_grad,
        shift_1_grad,
        flip(up_bias_full.reshape(up_rows, model)),
        bias_d_grad,
        gain_2_grad,
        shift_2_grad,
    ]
    vectors = [p for v in vectors for p in v.reshape(-1, model)]
    grad_step = -(-(quarter + tail + (len(vectors) + 1) // 2) // 16) * 16
    spare = grad_step - quarter - tail
    vectors = sum(
        jnp.pad(v[None], ((i, 2 * spare - 1 - i), (0, 0))) for i, v in enumerate(vectors)
    ).reshape(2, spare, model)

    grad_cols = exchange(attended_grad_t.reshape(tp_n, width, seqs * rows))

    def sum_ctx(x):
        for bit in reversed(ctx_bits):
            x = low(x)
            x = wide(x) + wide(swap(x, "ctx", bit))
        return x

    late_pre = after(pre_grad, attended_grad_t)
    ffn_grads = weight_grads(
        late_pre,
        hidden_low,
        activated,
        ffn_grad,
        attended_t,
        mixer_grad,
        vectors,
        ctx_n,
        tp_n,
        grad_step,
        tail,
    )
    ffn_sum = lax.psum_scatter(
        after(ffn_grads, grad_cols), ("ctx", "tp"), scatter_dimension=1, tiled=True
    )

    grad_rows = flip(grad_first).reshape(seqs, rows, model)
    spans = []
    for s in range(seqs):
        if s + 1 < seqs or heads == 1:
            spans.append((s, 0, heads))
        else:
            spans += [(s, 0, 1), (s, 1, heads - 1)]
    near = ctx_bits[-1:]
    far = list(reversed(ctx_bits[:-1]))

    def near_sum(keep, send):
        got = send
        for bit in near:
            got = swap(send, "ctx", bit)
        return [(keep[p], got[p]) if p == 0 else low(wide(keep[p]) + wide(got[p])) for p in range(half)]

    def far_sum(chunks):
        first, rest = chunks[0], chunks[1:]
        total = wide(first[0]) + wide(first[1])
        if len(far) == 1:
            return low(total + wide(swap(rest[0], "ctx", far[0])))
        chunks = [low(total)] + rest
        for bit in far:
            n = len(chunks) // 2
            chunks = [
                low(wide(a) + wide(swap(b, "ctx", bit))) for a, b in zip(chunks[:n], chunks[n:])
            ]
        return chunks[0]

    qkv_grad = 0.0
    sums = 0.0
    dq_parts = [[] for _ in range(seqs)]
    dkv_parts = [[] for _ in range(seqs)]
    last = ()
    near_chunks = None
    number = 0

    def finish(s, *gates):
        grads_t = jnp.concatenate(dq_parts[s] + dkv_parts[s], 0)
        back = low(dot(grads_t, qkv_t, TN))
        if gates:
            back = after(back, *gates)
        cut = back.reshape(tp_n, rows, model)
        if s + 1 < seqs:
            total = [lax.dynamic_index_in_dim(cut, tp_i, 0, False)] + [
                swap(lax.dynamic_index_in_dim(cut, tp_i ^ j, 0, False), "tp", j)
                for j in range(1, tp_n)
            ]
        else:
            total = [lax.psum_scatter(back, "tp", scatter_dimension=0, tiled=True)]
        return (
            back,
            total,
            dot(after(grads_t, back), blocks[s], NN),
            jnp.sum(wide(jnp.concatenate(dq_parts[s], 0)), axis=1),
        )

    def received(s, parts):
        total = grad_rows[s]
        for p in parts:
            total = total + wide(p)
        return low(total)

    moving = {}
    for s, start, count in spans:
        meta = metas[s]
        wait = list(last) if last else [grad_cols]
        if number >= 1:
            wait += near_chunks[1:]
        if number >= 2:
            done_s = spans[number - 2][0]
            wait.append(dkv_parts[done_s][-1])
            if spans[number - 1][0] != done_s:
                done = finish(done_s)
                wait.append(done[0])
                moving[done_s] = done[1]
                qkv_grad, sums = qkv_grad + done[2], sums + done[3]
        if wait:
            meta = after(meta, *wait)
        dq, keep, send = attend_backward(
            meta, queries[s], outs[s], grad_cols, totals[s], keys_values[s], rows, start, count, s
        )
        last = (dq,)
        number += 1
        if number > 1:
            before = spans[number - 2][0]
            keep, send, dkv_parts[before][-1] = lax.optimization_barrier(
                (keep, send, dkv_parts[before][-1])
            )
            for parts in moving.values():
                keep, send, parts[1:] = lax.optimization_barrier((keep, send, parts[1:]))
        near_chunks = near_sum(keep, send)
        dq_parts[s].append(dq)
        dkv_parts[s].append(far_sum(near_chunks))
    ffn_sum = low(scatter_local(ffn_sum.reshape(2 * grad_step, model)))
    done = finish(seqs - 1)
    moving[seqs - 1] = done[1]
    qkv_grad, sums = qkv_grad + done[2], sums + done[3]
    chunks = ctx_gather([ffn_sum])
    stacked = jnp.stack([chunks[ctx_order.index(e)] for e in range(ctx_n)], 0)
    stacked = xor_order(stacked, 0, ctx_i).reshape(ctx_n, 2, grad_step, part)
    summed = stacked[0, :, quarter + tail :].reshape(2 * spare, part)
    for i in range(tp_n.bit_length() - 1):
        summed = jnp.where((tp_i >> i) & 1 != 0, swap(summed, "tp", 1 << i), summed)
    summed = wide(flip(gather_local(summed)))
    stacked = wide(stacked)
    up_sum = stacked[:, 0, :quarter].reshape(units, part)
    down_sum = stacked[:, 1, :quarter].reshape(units, part)
    out_sum = stacked[:, :, quarter : quarter + tail].reshape(width, part)

    if two:
        sums = jnp.pad(sums, (0, part - width))
        sums = jnp.pad(jnp.concatenate([sums, sums])[None], ((0, 15), (0, 0)))
        qkv_sum = scatter_local(flip(low(jnp.concatenate([qkv_grad, sums], 0))))
        qkv_sum = sum_ctx(after(qkv_sum, ffn_sum))
        query_bias_sum = qkv_sum[3 * width, :width]
    else:
        qkv_sum = sum_ctx(scatter_local(low(qkv_grad)))
        query_bias_sum = lax.psum(sums, ("shard", "ctx"))
    query_sum = qkv_sum[:width]
    kv_sum = qkv_sum[width : 3 * width].reshape(heads, 2, HD, part)
    key_sum = kv_sum[:, 0].reshape(width, part)
    value_sum = kv_sum[:, 1].reshape(width, part)

    query_bias_parts = [query_bias_sum] + [swap(query_bias_sum, "tp", j) for j in range(1, tp_n)]
    query_bias_full = xor_order(jnp.stack(query_bias_parts, 0), 0, tp_i).reshape(-1)
    moving[seqs - 1][0] = after(moving[seqs - 1][0], query_bias_full, qkv_sum, out_sum, summed)
    input_grads = jnp.stack([received(s, moving[s]) for s in range(seqs)], 0)
    ends = [*summed[:4], summed[4 : 4 + up_rows].reshape(-1), *summed[4 + up_rows : 7 + up_rows]]
    return (
        low(flip(result)).reshape(seqs, rows, model),
        input_grads,
        query_sum.T,
        query_bias_full,
        key_sum.T,
        value_sum.T,
        ends[0],
        out_sum,
        ends[1],
        ends[2],
        ends[3],
        up_sum.T,
        ends[4],
        down_sum,
        ends[5],
        ends[6],
        ends[7],
    )


def solution(mesh):
    placed = (
        P("shard", ("ctx", "tp"), None),
        P("shard", ("ctx", "tp"), None),
        P("shard"),
        P("shard", "tp"),
        P("tp"),
        P("shard", "tp"),
        P("shard", "tp"),
        P("tp"),
        P("tp", "shard"),
        P(),
        P(),
        P(),
        P("shard", "tp"),
        P("tp"),
        P("tp", "shard"),
        P(),
        P(),
        P(),
    )
    return jax.shard_map(
        on_device,
        mesh=mesh,
        in_specs=placed,
        out_specs=(
            P("shard", ("ctx", "tp"), None),
            P("shard", ("ctx", "tp"), None),
            P("shard", "tp"),
            P(),
            P("shard", "tp"),
            P("shard", "tp"),
            P(),
            P("tp", "shard"),
            P(),
            P(),
            P(),
            P("shard", "tp"),
            P(),
            P("tp", "shard"),
            P(),
            P(),
            P(),
        ),
        check_vma=False,
    )
```

```python
import functools

import jax
import jax.numpy as jnp
from jax import lax
from jax.experimental import pallas as pl
from jax.experimental.pallas import tpu as pltpu
from jax.sharding import PartitionSpec as P

HD = 64
EXT = 128
VE = 80
epsilon = 1e-12
f32 = jnp.float32
bf16 = jnp.bfloat16


def extended(block, extra_rows):
    n = block.shape[1]
    row = lax.broadcasted_iota(jnp.int32, (EXT - HD, n), 0)
    extra = jnp.zeros((EXT - HD, n), f32)
    for place, values in enumerate(extra_rows):
        extra = jnp.where(row == place, values, extra)
    return jnp.concatenate([block, extra.astype(bf16)], axis=0)


def key_bias(meta, block, size, blocks):
    count = meta[1 + blocks + block]
    lane = lax.broadcasted_iota(jnp.int32, (1, size), 1)
    return jnp.where(lane < count, 0.0, -1e30).astype(f32)


def block_loops(count, step, long, short):
    def long_step(i, carry):
        step(i * long, long)
        return carry

    def short_step(i, carry):
        step(whole * long + i * short, short)
        return carry

    whole = count // long
    lax.fori_loop(0, whole, long_step, 0)
    lax.fori_loop(0, (count - whole * long + short - 1) // short, short_step, 0)


def forward_kernel(meta, qt, *refs, size, pieces, inner, long, short):
    kv = refs[:pieces]
    ot, lse, key_rows, value_cols, acc, top = refs[pieces:]
    blocks = pieces * inner
    n = qt.shape[1]
    one = jnp.ones((1, size), f32)
    for e in range(pieces):
        for j in range(inner):
            b = e * inner + j
            here = slice(j * size, (j + 1) * size)
            there = slice(b * size, (b + 1) * size)
            bias = key_bias(meta, b, size, blocks)
            key_rows[there, :] = extended(kv[e][:HD, here], [bias]).T
            value_cols[:, there] = extended(kv[e][HD:, here], [one])[:VE]
    queries = extended(qt[...], [jnp.ones((1, n), f32)])
    acc[...] = jnp.zeros_like(acc)
    top[...] = jnp.full_like(top, -1e30)

    def step(first, unroll):
        starts = [pl.multiple_of(meta[1 + first + u] * size, size) for u in range(unroll)]
        scores = [
            jnp.dot(key_rows[pl.ds(s, size), :], queries, preferred_element_type=f32)
            for s in starts
        ]
        old = top[...]
        new = old
        for s in scores:
            new = jnp.maximum(new, jnp.max(s, axis=0, keepdims=True))
        total = acc[...] * jnp.exp(old - new)
        for s, start in zip(scores, starts):
            probs = jnp.exp(s - new).astype(bf16)
            total = total + jnp.dot(
                value_cols[:, pl.ds(start, size)], probs, preferred_element_type=f32
            )
        acc[...] = total
        top[...] = new

    block_loops(meta[0], step, long, short)
    exp_total = acc[HD : HD + 1, :]
    out = (acc[:HD, :] / exp_total).astype(bf16)
    for j in range(ot.shape[0]):
        ot[j] = out[:, j * ot.shape[2] : (j + 1) * ot.shape[2]]
    lse[0] = top[...] + jnp.log(exp_total)


def backward_kernel(meta, qt, ot, dot_t, lse, *refs, size, pieces, inner, long, short):
    kv = refs[:pieces]
    dq, keep, send = refs[pieces : pieces + 3]
    key_cols, value_cols, key_rows, query_rows, grad_rows, grad_cols, dq_acc, both = refs[
        pieces + 3 :
    ]
    blocks = pieces * inner
    half = keep.shape[0]
    n = qt.shape[1]
    one = jnp.ones((1, size), f32)
    for e in range(pieces):
        for j in range(inner):
            b = e * inner + j
            here = slice(j * size, (j + 1) * size)
            there = slice(b * size, (b + 1) * size)
            bias = key_bias(meta, b, size, blocks)
            keys = extended(kv[e][:HD, here], [bias, one, one, one])
            key_cols[:, there] = keys
            key_rows[there, :] = keys.T
            value_cols[:, there] = extended(kv[e][HD:, here], [one, one])
    minus = -lse[0]
    high = minus.astype(bf16).astype(f32)
    mid = (minus - high).astype(bf16).astype(f32)
    query_rows[...] = extended(qt[...], [jnp.ones((1, n), f32), high, mid, minus - high - mid]).T
    grads = jnp.concatenate([dot_t[j] for j in range(dot_t.shape[0])], 1)
    outs = jnp.concatenate([ot[j] for j in range(ot.shape[0])], 1)
    grad_cols[...] = grads
    row_dot = -jnp.sum(grads.astype(f32) * outs.astype(f32), axis=0, keepdims=True)
    high = row_dot.astype(bf16).astype(f32)
    grad_rows[...] = extended(grads, [high, row_dot - high]).T
    dq_acc[...] = jnp.zeros_like(dq_acc)
    both[...] = jnp.zeros_like(both)

    def step(first, unroll):
        score_grads, rows, found = [], [], []
        for u in range(unroll):
            b = meta[1 + first + u]
            start = pl.multiple_of(b * size, size)
            probs = jnp.exp(
                jnp.dot(
                    query_rows[...], key_cols[:, pl.ds(start, size)], preferred_element_type=f32
                )
            )
            centred = jnp.dot(
                grad_rows[...], value_cols[:, pl.ds(start, size)], preferred_element_type=f32
            )
            score_grad = (probs * centred).astype(bf16)
            score_grads.append(score_grad)
            rows.append(key_rows[pl.ds(start, size), :])
            dk = jnp.dot(qt[...], score_grad, preferred_element_type=f32)
            dv = jnp.dot(grad_cols[...], probs.astype(bf16), preferred_element_type=f32)
            found.append((b, dk.astype(bf16), dv.astype(bf16)))
        dq_acc[...] += jnp.dot(
            jnp.concatenate(score_grads, 1),
            jnp.concatenate(rows, 0),
            preferred_element_type=f32,
        )
        for b, dk, dv in found:
            lane = pl.multiple_of((b % inner) * size, size)
            both[b // inner, :HD, pl.ds(lane, size)] = dk
            both[b // inner, HD:, pl.ds(lane, size)] = dv

    block_loops(meta[0], step, long, short)
    keep[...] = both[:half]
    send[...] = both[half:]
    dq[...] = (dq_acc[...].T[:HD] * HD ** (-0.5)).astype(bf16)


def unrolled(blocks, most):
    return (most, 2) if blocks % most == 0 else (1, 1)


def attend_forward(meta, qt, kvs, size, first, count):
    n, pieces = qt.shape[1], len(kvs)
    columns = kvs[0].shape[1]
    inner = columns // size
    keys = pieces * columns
    long, short = unrolled(pieces * inner, 8)
    return pl.pallas_call(
        functools.partial(
            forward_kernel, size=size, pieces=pieces, inner=inner, long=long, short=short
        ),
        grid_spec=pltpu.PrefetchScalarGridSpec(
            num_scalar_prefetch=1,
            grid=(count,),
            in_specs=[pl.BlockSpec((HD, n), lambda h, m: (first + h, 0))]
            + [pl.BlockSpec((2 * HD, columns), lambda h, m: (first + h, 0))] * pieces,
            out_specs=[
                pl.BlockSpec((n // size, HD, size), lambda h, m: (0, h, 0)),
                pl.BlockSpec((1, 1, n), lambda h, m: (h, 0, 0)),
            ],
            scratch_shapes=[
                pltpu.VMEM((keys, EXT), bf16),
                pltpu.VMEM((VE, keys), bf16),
                pltpu.VMEM((VE, n), f32),
                pltpu.VMEM((1, n), f32),
            ],
        ),
        out_shape=[
            jax.ShapeDtypeStruct((n // size, count * HD, size), bf16),
            jax.ShapeDtypeStruct((count, 1, n), f32),
        ],
        cost_estimate=pl.CostEstimate(
            flops=20 * count * HD * n * keys,
            bytes_accessed=8 * count * HD * n,
            transcendentals=0,
        ),
        name="attend_forward",
    )(meta, qt, *kvs)


def attend_backward(meta, qt, ot, dot_t, lse, kvs, size, first, count, seq):
    n, pieces = qt.shape[1], len(kvs)
    columns = kvs[0].shape[1]
    inner = columns // size
    keys = pieces * columns
    half = (pieces + 1) // 2
    long, short = unrolled(pieces * inner, 4)
    row_spec = pl.BlockSpec((HD, n), lambda h, m: (first + h, 0))
    split_spec = pl.BlockSpec((n // size, HD, size), lambda h, m: (0, first + h, 0))
    grad_spec = pl.BlockSpec((n // size, HD, size), lambda h, m: (0, first + h, seq))
    part_spec = pl.BlockSpec((half, 2 * HD, columns), lambda h, m: (0, h, 0))
    part_shape = jax.ShapeDtypeStruct((half, 2 * HD * count, columns), bf16)
    return pl.pallas_call(
        functools.partial(
            backward_kernel, size=size, pieces=pieces, inner=inner, long=long, short=short
        ),
        grid_spec=pltpu.PrefetchScalarGridSpec(
            num_scalar_prefetch=1,
            grid=(count,),
            in_specs=[row_spec, split_spec, grad_spec]
            + [pl.BlockSpec((1, 1, n), lambda h, m: (first + h, 0, 0))]
            + [pl.BlockSpec((2 * HD, columns), lambda h, m: (first + h, 0))] * pieces,
            out_specs=[pl.BlockSpec((HD, n), lambda h, m: (h, 0)), part_spec, part_spec],
            scratch_shapes=[
                pltpu.VMEM((EXT, keys), bf16),
                pltpu.VMEM((EXT, keys), bf16),
                pltpu.VMEM((keys, EXT), bf16),
                pltpu.VMEM((n, EXT), bf16),
                pltpu.VMEM((n, EXT), bf16),
                pltpu.VMEM((HD, n), bf16),
                pltpu.VMEM((n, EXT), f32),
                pltpu.VMEM((pieces, 2 * HD, columns), bf16),
            ],
        ),
        out_shape=[jax.ShapeDtypeStruct((count * HD, n), bf16), part_shape, part_shape],
        cost_estimate=pl.CostEstimate(
            flops=count * HD * n,
            bytes_accessed=count * HD * n,
            transcendentals=0,
        ),
        name="attend_backward",
    )(meta, qt, ot, dot_t, lse, *kvs)


def weight_grad_kernel(
    pre, hidden, act, grad, mixed_t, mixer, vectors, out, mixed_sum, *, tp_n, step, tail
):
    half, piece = pl.program_id(0), pl.program_id(1)

    @pl.when((half == 0) & (piece == 0))
    def _():
        mixed_sum[...] = jnp.dot(mixed_t[...], mixer[...], preferred_element_type=f32)

    quarter = pre.shape[1] // tp_n

    def fill(left, right):
        found = lax.dot_general(
            left, right, (((0,), (0,)), ((), ())), preferred_element_type=f32
        ).astype(bf16)
        for t in range(tp_n):
            out[0, t * step : t * step + quarter, :] = found[t * quarter : (t + 1) * quarter]

    @pl.when(half == 0)
    def _():
        fill(pre[...], hidden[...])

    @pl.when(half == 1)
    def _():
        fill(act[...], grad[...])

    width = mixed_sum.shape[0] // tp_n
    for t in range(tp_n):
        start = pl.multiple_of(t * width + (piece * 2 + half) * tail, 8)
        ending = jnp.concatenate([mixed_sum[pl.ds(start, tail), :], vectors[half]], 0)
        out[0, t * step + quarter : (t + 1) * step, :] = ending.astype(bf16)


def weight_grads(pre, hidden, act, grad, mixed_t, mixer, vectors, pieces, tp_n, step, tail):
    n, columns = pre.shape
    width = hidden.shape[1]
    tile = columns // pieces
    whole = lambda x: pl.BlockSpec(x.shape, lambda g, i: (0, 0))
    return pl.pallas_call(
        functools.partial(weight_grad_kernel, tp_n=tp_n, step=step, tail=tail),
        grid=(2, pieces),
        in_specs=[
            pl.BlockSpec((n, tile), lambda g, i: (0, i * (1 - g) + (pieces - 1) * g)),
            whole(hidden),
            pl.BlockSpec((n, tile), lambda g, i: (0, i * g)),
            whole(grad),
            whole(mixed_t),
            whole(mixer),
            pl.BlockSpec(vectors.shape, lambda g, i: (0, 0, 0)),
        ],
        out_specs=pl.BlockSpec((1, tp_n * step, width), lambda g, i: (g, i, 0)),
        out_shape=jax.ShapeDtypeStruct((2, pieces * tp_n * step, width), bf16),
        scratch_shapes=[pltpu.VMEM((mixed_t.shape[0], width), f32)],
        cost_estimate=pl.CostEstimate(
            flops=4 * n * columns * width, bytes_accessed=8 * n * columns, transcendentals=0
        ),
        name="weight_grads",
    )(pre, hidden, act, grad, mixed_t, mixer, vectors)


def swap(x, axis, bits):
    return lax.ppermute(x, axis, [(i, i ^ bits) for i in range(lax.axis_size(axis))])


def wide(x):
    return x.astype(f32)


def low(x):
    return x.astype(bf16)


def dot(a, b, contract):
    return lax.dot_general(a, b, (contract, ((), ())), preferred_element_type=f32)


NN = ((1,), (0,))
NT = ((1,), (1,))
TN = ((0,), (0,))


def xor_order(x, axis, index):
    n = x.shape[axis]
    bit = 1
    while bit < n:
        moved = jnp.stack([lax.index_in_dim(x, i ^ bit, axis, False) for i in range(n)], axis)
        x = jnp.where((index & bit) != 0, moved, x)
        bit *= 2
    return x


def norm_forward(resid, gain, shift):
    centre = resid - jnp.mean(resid, axis=-1, keepdims=True)
    factor = lax.rsqrt(jnp.mean(centre * centre, axis=-1, keepdims=True) + epsilon)
    normed = centre * factor
    return (normed * gain + shift, normed, factor)


def norm_backward(grad_out, normed, factor, gain):
    scaled = grad_out * gain
    centred = scaled - jnp.mean(scaled, axis=-1, keepdims=True)
    return factor * (centred - normed * jnp.mean(scaled * normed, axis=-1, keepdims=True))


def on_device(
    tokens,
    cotangent,
    lengths,
    query_weight,
    query_bias,
    key_weight,
    value_weight,
    value_bias,
    out_weight,
    out_bias,
    first_gain,
    first_shift,
    up_weight,
    up_bias,
    down_weight,
    down_bias,
    second_gain,
    second_shift,
):
    shard_n, ctx_n, tp_n = (lax.axis_size(a) for a in ("shard", "ctx", "tp"))
    shard_i, ctx_i, tp_i = (lax.axis_index(a) for a in ("shard", "ctx", "tp"))
    seqs, rows, model = tokens.shape
    part = model // shard_n
    width = query_weight.shape[1]
    heads = width // HD
    units = up_weight.shape[1]
    quarter = units // ctx_n
    two = shard_n == 2
    first = shard_i == 0

    def flip(x):
        if not two:
            return x
        return jnp.where(first, x, jnp.concatenate([x[..., part:], x[..., :part]], -1))

    def gather_local(x):
        if two:
            return jnp.concatenate([x, swap(x, "shard", 1)], -1)
        return lax.all_gather(x, "shard", axis=x.ndim - 1, tiled=True)

    def scatter_local(x):
        if two:
            return wide(x[:, :part]) + wide(swap(x[:, part:], "shard", 1))
        return wide(lax.psum_scatter(x, "shard", scatter_dimension=1, tiled=True))

    def after(x, *gates):
        return lax.optimization_barrier((x, *gates))[0]

    bits = ctx_n.bit_length() - 1
    ctx_bits = [1 << i for i in reversed(range(bits))]

    def bit_reverse(e):
        return sum(((e >> i) & 1) << (bits - 1 - i) for i in range(bits))

    ctx_order = [bit_reverse(e) for e in range(ctx_n)]
    half = (ctx_n + 1) // 2

    def exchange(x):
        return lax.all_to_all(x, "tp", 0, 0, tiled=True)

    def tp_gather(x):
        return exchange(jnp.broadcast_to(x[None], (tp_n, *x.shape)))

    def ctx_gather(chunks, some=None):
        for bit in ctx_bits if some is None else some:
            chunks = chunks + [swap(c, "ctx", bit) for c in chunks]
        return chunks

    kv_t = jnp.stack(
        [key_weight.T.reshape(heads, HD, part), value_weight.T.reshape(heads, HD, part)], 1
    ).reshape(2 * width, part)
    mine = lambda w: lax.dynamic_slice_in_dim(w, ctx_i * quarter, quarter, 0)
    qkv_t = flip(gather_local(jnp.concatenate([query_weight.T, kv_t], 0)))
    kv_bias = jnp.stack(
        [jnp.zeros((heads, HD), f32), value_bias.reshape(heads, HD)], 1
    ).reshape(2 * width, 1)

    first_in = tp_gather(tokens[0])
    blocks = [first_in.reshape(tp_n * rows, model)]
    for s in range(1, seqs):
        blocks.append(tp_gather(after(tokens[s], blocks[-1])).reshape(tp_n * rows, model))

    bias_rows = []
    rest = up_bias
    for _ in range(3):
        bias_rows.append(low(rest))
        rest = rest - wide(bias_rows[-1])
    extra = 3 * units // model
    bias_rows = jnp.stack(bias_rows, 0).reshape(extra, model)
    bias_rows = lax.dynamic_slice_in_dim(bias_rows, shard_i * part, part, 1)
    tail = width // ctx_n // 2
    step = -(-(quarter + tail + extra) // 16) * 16
    out_mine = lax.dynamic_slice_in_dim(out_weight, ctx_i * 2 * tail, 2 * tail, 0)
    fill = jnp.zeros((step - quarter - tail - extra, part), bf16)
    pack = jnp.stack(
        [
            jnp.concatenate([mine(up_weight.T), bias_rows, fill, out_mine[:tail]], 0),
            jnp.concatenate(
                [mine(down_weight), jnp.zeros((extra, part), bf16), fill, out_mine[tail:]], 0
            ),
        ],
        0,
    )
    pack = lax.all_gather(after(pack, blocks[-1]), "tp", axis=1, tiled=True)
    chunk = tp_n * step
    ups = [gather_local(pack[0])]
    downs = after(jnp.concatenate(ctx_gather([pack[1]], ctx_bits[:-1]), 0), *ups)

    place = jnp.arange(ctx_n * tp_n)
    order = bit_reverse((place // tp_n) ^ ctx_i) * tp_n + place % tp_n
    block_at = (bit_reverse(place // tp_n) ^ ctx_i) * tp_n + place % tp_n

    def project(s, block):
        kv = low(dot(qkv_t[width:], block, NT) + kv_bias)
        q = low(dot(qkv_t[:width], block, NT) + query_bias[:, None])
        return kv, q * bf16(HD ** (-0.5))

    def ctx_pieces(kv, gate):
        chunks = [kv]
        for bit in ctx_bits:
            chunks = chunks + [swap(c, "ctx", bit) for c in chunks]
            if gate is not None and bit == ctx_bits[0]:
                chunks = [after(c, gate) for c in chunks]
        return chunks

    metas = []
    for s in range(seqs):
        count = jnp.clip(lengths[s] - block_at * rows, 0, rows)
        metas.append(
            jnp.concatenate([((lengths[s] + rows - 1) // rows)[None], order, count]).astype(
                jnp.int32
            )
        )

    outs, totals, attended, queries, keys_values = [], [], [], [], []
    kv, q = project(0, blocks[0])
    kvs = ctx_pieces(kv, None)
    for s in range(seqs):
        keys_values.append(kvs)
        queries.append(q)
        if s + 1 < seqs and heads > 1:
            ot_a, lse_a = attend_forward(metas[s], q, kvs, rows, 0, heads - 1)
            kv_next, q_next = project(s + 1, after(blocks[s + 1], lse_a))
            meta = after(metas[s], kv_next, q_next)
            ot_b, lse_b = attend_forward(meta, q, kvs, rows, heads - 1, 1)
            ot = jnp.concatenate([ot_a, ot_b], 1)
            lse = jnp.concatenate([lse_a, lse_b], 0)
            q, kvs = q_next, ctx_pieces(kv_next, lse_b)
        else:
            ot_a, lse_a = attend_forward(metas[s], q, kvs, rows, 0, heads - 1)
            meta = after(metas[s], lse_a, ups[0], downs)
            ot_b, lse_b = attend_forward(meta, q, kvs, rows, heads - 1, 1)
            ot = jnp.concatenate([ot_a, ot_b], 1)
            lse = jnp.concatenate([lse_a, lse_b], 0)
        outs.append(ot)
        totals.append(lse)
        attended.append(exchange(ot).reshape(tp_n * width, rows))
    ups = ctx_gather(ups)
    downs = after(gather_local(downs), attended[-1])
    downs = [downs[i * chunk : (i + 1) * chunk] for i in range(half)]
    downs = ctx_gather(downs, ctx_bits[-1:])

    def natural(pieces):
        whole = jnp.zeros((ctx_n, *pieces[0].shape), bf16)
        for e, piece in zip(ctx_order, pieces):
            whole = lax.dynamic_update_slice_in_dim(whole, piece[None], e ^ ctx_i, 0)
        return whole

    ups = [x.reshape(tp_n, step, model) for x in ups]
    downs = [x.reshape(tp_n, step, model) for x in downs]
    up_full = natural([x[:, :quarter] for x in ups]).reshape(-1, model)
    down_full = natural([x[:, :quarter] for x in downs]).reshape(-1, model)
    ends = [
        jnp.stack([x[:, step - tail :] for x in pair], 1) for pair in zip(ups, downs)
    ]
    out_full = natural(ends).transpose(1, 0, 2, 3, 4).reshape(tp_n * width, model)
    unit_bias = wide(flip(ups[0][:, quarter : quarter + extra]))
    unit_bias = unit_bias.reshape(tp_n, 3, ctx_n, quarter)
    unit_bias = (unit_bias[:, 0] + unit_bias[:, 1]) + unit_bias[:, 2]
    unit_bias = unit_bias.transpose(1, 0, 2).reshape(1, ctx_n * tp_n * quarter)

    attended_t = jnp.concatenate(attended, 1)

    flat = flip(wide(tokens.reshape(seqs * rows, model)))
    cot = flip(wide(cotangent.reshape(seqs * rows, model)))
    gain_1, shift_1, gain_2, shift_2, bias_o, bias_d = (
        flip(v) for v in (first_gain, first_shift, second_gain, second_shift, out_bias, down_bias)
    )
    mixed = dot(attended_t, out_full, TN) + bias_o
    hidden, normed_1, factor_1 = norm_forward(flat + mixed, gain_1, shift_1)
    hidden_low = low(hidden)
    pre = dot(hidden_low, up_full, NT) + unit_bias
    share = 0.5 * (1.0 + lax.erf(pre * 0.5**0.5))
    activated = low(pre * share)
    slope = low(share + pre * jnp.exp(-0.5 * pre * pre) * 0.3989422804014327)
    ffn_out = dot(activated, down_full, NN) + bias_d
    result, normed_2, factor_2 = norm_forward(hidden + ffn_out, gain_2, shift_2)
    here = (ctx_i * tp_n + tp_i) * rows + jnp.arange(rows)
    valid = (here[None, :] < lengths[:, None]).reshape(seqs * rows, 1)
    grad_result = jnp.where(valid, cot, 0.0)
    gain_2_grad = jnp.sum(grad_result * normed_2, axis=0)
    shift_2_grad = jnp.sum(grad_result, axis=0)
    grad_second = norm_backward(grad_result, normed_2, factor_2, gain_2)
    ffn_grad = low(grad_second)
    bias_d_grad = jnp.sum(wide(ffn_grad), axis=0)
    pre_grad = low(dot(ffn_grad, down_full, NT) * wide(slope))
    grad_hidden = grad_second + dot(pre_grad, up_full, NN)
    up_bias_grad = jnp.sum(wide(pre_grad), axis=0)
    gain_1_grad = jnp.sum(grad_hidden * normed_1, axis=0)
    shift_1_grad = jnp.sum(grad_hidden, axis=0)
    grad_first = norm_backward(grad_hidden, normed_1, factor_1, gain_1)
    mixer_grad = low(grad_first)
    bias_o_grad = jnp.sum(wide(mixer_grad), axis=0)
    attended_grad_t = low(dot(out_full, mixer_grad, NT))
    value_bias_parts = jnp.sum(
        wide(attended_grad_t).reshape(tp_n, width, seqs * rows), axis=2
    )
    value_bias_grad = value_bias_parts.reshape(-1)
    up_bias_full = up_bias_grad.reshape(ctx_n, tp_n, quarter).transpose(1, 0, 2).reshape(-1)
    up_rows = up_bias_full.shape[0] // model
    vectors = [
        flip(value_bias_grad),
        bias_o_grad,
        gain_1_grad,
        shift_1_grad,
        flip(up_bias_full.reshape(up_rows, model)),
        bias_d_grad,
        gain_2_grad,
        shift_2_grad,
    ]
    vectors = [p for v in vectors for p in v.reshape(-1, model)]
    grad_step = -(-(quarter + tail + (len(vectors) + 1) // 2) // 16) * 16
    spare = grad_step - quarter - tail
    vectors = sum(
        jnp.pad(v[None], ((i, 2 * spare - 1 - i), (0, 0))) for i, v in enumerate(vectors)
    ).reshape(2, spare, model)

    grad_cols = exchange(attended_grad_t.reshape(tp_n, width, seqs * rows))

    def sum_ctx(x):
        for bit in reversed(ctx_bits):
            x = low(x)
            x = wide(x) + wide(swap(x, "ctx", bit))
        return x

    late_pre = after(pre_grad, attended_grad_t)
    ffn_grads = weight_grads(
        late_pre,
        hidden_low,
        activated,
        ffn_grad,
        attended_t,
        mixer_grad,
        vectors,
        ctx_n,
        tp_n,
        grad_step,
        tail,
    )
    ffn_sum = lax.psum_scatter(
        after(ffn_grads, grad_cols), ("ctx", "tp"), scatter_dimension=1, tiled=True
    )

    grad_rows = flip(grad_first).reshape(seqs, rows, model)
    spans = []
    for s in range(seqs):
        if s + 1 < seqs or heads == 1:
            spans.append((s, 0, heads))
        else:
            spans += [(s, 0, 1), (s, 1, heads - 1)]
    near = ctx_bits[-1:]
    far = list(reversed(ctx_bits[:-1]))

    def near_sum(keep, send):
        got = send
        for bit in near:
            got = swap(send, "ctx", bit)
        return [(keep[p], got[p]) if p == 0 else low(wide(keep[p]) + wide(got[p])) for p in range(half)]

    def far_sum(chunks):
        first, rest = chunks[0], chunks[1:]
        total = wide(first[0]) + wide(first[1])
        if len(far) == 1:
            return low(total + wide(swap(rest[0], "ctx", far[0])))
        chunks = [low(total)] + rest
        for bit in far:
            n = len(chunks) // 2
            chunks = [
                low(wide(a) + wide(swap(b, "ctx", bit))) for a, b in zip(chunks[:n], chunks[n:])
            ]
        return chunks[0]

    qkv_grad = 0.0
    sums = 0.0
    dq_parts = [[] for _ in range(seqs)]
    dkv_parts = [[] for _ in range(seqs)]
    last = ()
    near_chunks = None
    number = 0

    def finish(s, *gates):
        grads_t = jnp.concatenate(dq_parts[s] + dkv_parts[s], 0)
        back = low(dot(grads_t, qkv_t, TN))
        if gates:
            back = after(back, *gates)
        cut = back.reshape(tp_n, rows, model)
        if s + 1 < seqs:
            total = [lax.dynamic_index_in_dim(cut, tp_i, 0, False)] + [
                swap(lax.dynamic_index_in_dim(cut, tp_i ^ j, 0, False), "tp", j)
                for j in range(1, tp_n)
            ]
        else:
            total = [lax.psum_scatter(back, "tp", scatter_dimension=0, tiled=True)]
        return (
            back,
            total,
            dot(after(grads_t, back), blocks[s], NN),
            jnp.sum(wide(jnp.concatenate(dq_parts[s], 0)), axis=1),
        )

    def received(s, parts):
        total = grad_rows[s]
        for p in parts:
            total = total + wide(p)
        return low(total)

    moving = {}
    for s, start, count in spans:
        meta = metas[s]
        wait = list(last) if last else [grad_cols]
        if number >= 1:
            wait += near_chunks[1:]
        if number >= 2:
            done_s = spans[number - 2][0]
            wait.append(dkv_parts[done_s][-1])
            if spans[number - 1][0] != done_s:
                done = finish(done_s)
                wait.append(done[0])
                moving[done_s] = done[1]
                qkv_grad, sums = qkv_grad + done[2], sums + done[3]
        if wait:
            meta = after(meta, *wait)
        dq, keep, send = attend_backward(
            meta, queries[s], outs[s], grad_cols, totals[s], keys_values[s], rows, start, count, s
        )
        last = (dq,)
        number += 1
        if number > 1:
            before = spans[number - 2][0]
            keep, send, dkv_parts[before][-1] = lax.optimization_barrier(
                (keep, send, dkv_parts[before][-1])
            )
            for parts in moving.values():
                keep, send, parts[1:] = lax.optimization_barrier((keep, send, parts[1:]))
        near_chunks = near_sum(keep, send)
        dq_parts[s].append(dq)
        dkv_parts[s].append(far_sum(near_chunks))
    ffn_sum = low(scatter_local(ffn_sum.reshape(2 * grad_step, model)))
    done = finish(seqs - 1)
    moving[seqs - 1] = done[1]
    qkv_grad, sums = qkv_grad + done[2], sums + done[3]
    chunks = ctx_gather([ffn_sum])
    stacked = jnp.stack([chunks[ctx_order.index(e)] for e in range(ctx_n)], 0)
    stacked = xor_order(stacked, 0, ctx_i).reshape(ctx_n, 2, grad_step, part)
    summed = stacked[0, :, quarter + tail :].reshape(2 * spare, part)
    for i in range(tp_n.bit_length() - 1):
        summed = jnp.where((tp_i >> i) & 1 != 0, swap(summed, "tp", 1 << i), summed)
    summed = wide(flip(gather_local(summed)))
    stacked = wide(stacked)
    up_sum = stacked[:, 0, :quarter].reshape(units, part)
    down_sum = stacked[:, 1, :quarter].reshape(units, part)
    out_sum = stacked[:, :, quarter : quarter + tail].reshape(width, part)

    if two:
        sums = jnp.pad(sums, (0, part - width))
        sums = jnp.pad(jnp.concatenate([sums, sums])[None], ((0, 15), (0, 0)))
        qkv_sum = scatter_local(flip(low(jnp.concatenate([qkv_grad, sums], 0))))
        qkv_sum = sum_ctx(after(qkv_sum, ffn_sum))
        query_bias_sum = qkv_sum[3 * width, :width]
    else:
        qkv_sum = sum_ctx(scatter_local(low(qkv_grad)))
        query_bias_sum = lax.psum(sums, ("shard", "ctx"))
    query_sum = qkv_sum[:width]
    kv_sum = qkv_sum[width : 3 * width].reshape(heads, 2, HD, part)
    key_sum = kv_sum[:, 0].reshape(width, part)
    value_sum = kv_sum[:, 1].reshape(width, part)

    query_bias_parts = [query_bias_sum] + [swap(query_bias_sum, "tp", j) for j in range(1, tp_n)]
    query_bias_full = xor_order(jnp.stack(query_bias_parts, 0), 0, tp_i).reshape(-1)
    moving[seqs - 1][0] = after(moving[seqs - 1][0], query_bias_full, qkv_sum, out_sum, summed)
    input_grads = jnp.stack([received(s, moving[s]) for s in range(seqs)], 0)
    ends = [*summed[:4], summed[4 : 4 + up_rows].reshape(-1), *summed[4 + up_rows : 7 + up_rows]]
    return (
        low(flip(result)).reshape(seqs, rows, model),
        input_grads,
        query_sum.T,
        query_bias_full,
        key_sum.T,
        value_sum.T,
        ends[0],
        out_sum,
        ends[1],
        ends[2],
        ends[3],
        up_sum.T,
        ends[4],
        down_sum,
        ends[5],
        ends[6],
        ends[7],
    )


def solution(mesh):
    placed = (
        P("shard", ("ctx", "tp"), None),
        P("shard", ("ctx", "tp"), None),
        P("shard"),
        P("shard", "tp"),
        P("tp"),
        P("shard", "tp"),
        P("shard", "tp"),
        P("tp"),
        P("tp", "shard"),
        P(),
        P(),
        P(),
        P("shard", "tp"),
        P("tp"),
        P("tp", "shard"),
        P(),
        P(),
        P(),
    )
    return jax.shard_map(
        on_device,
        mesh=mesh,
        in_specs=placed,
        out_specs=(
            P("shard", ("ctx", "tp"), None),
            P("shard", ("ctx", "tp"), None),
            P("shard", "tp"),
            P(),
            P("shard", "tp"),
            P("shard", "tp"),
            P(),
            P("tp", "shard"),
            P(),
            P(),
            P(),
            P("shard", "tp"),
            P(),
            P("tp", "shard"),
            P(),
            P(),
            P(),
        ),
        check_vma=False,
    )
```

```python
import functools

import jax
import jax.numpy as jnp
from jax import lax
from jax.experimental import pallas as pl
from jax.experimental.pallas import tpu as pltpu
from jax.sharding import PartitionSpec as P

HD = 64
EXT = 128
VE = 80
epsilon = 1e-12
f32 = jnp.float32
bf16 = jnp.bfloat16


def extended(block, extra_rows):
    n = block.shape[1]
    row = lax.broadcasted_iota(jnp.int32, (EXT - HD, n), 0)
    extra = jnp.zeros((EXT - HD, n), f32)
    for place, values in enumerate(extra_rows):
        extra = jnp.where(row == place, values, extra)
    return jnp.concatenate([block, extra.astype(bf16)], axis=0)


def key_bias(meta, block, size, blocks):
    count = meta[1 + blocks + block]
    lane = lax.broadcasted_iota(jnp.int32, (1, size), 1)
    return jnp.where(lane < count, 0.0, -1e30).astype(f32)


def block_loops(count, step, long, short):
    def long_step(i, carry):
        step(i * long, long)
        return carry

    def short_step(i, carry):
        step(whole * long + i * short, short)
        return carry

    whole = count // long
    lax.fori_loop(0, whole, long_step, 0)
    lax.fori_loop(0, (count - whole * long + short - 1) // short, short_step, 0)


def forward_kernel(meta, qt, *refs, size, pieces, inner, long, short):
    kv = refs[:pieces]
    ot, lse, key_rows, value_cols, acc, top = refs[pieces:]
    blocks = pieces * inner
    n = qt.shape[1]
    one = jnp.ones((1, size), f32)
    for e in range(pieces):
        for j in range(inner):
            b = e * inner + j
            here = slice(j * size, (j + 1) * size)
            there = slice(b * size, (b + 1) * size)
            bias = key_bias(meta, b, size, blocks)
            key_rows[there, :] = extended(kv[e][:HD, here], [bias]).T
            value_cols[:, there] = extended(kv[e][HD:, here], [one])[:VE]
    queries = extended(qt[...], [jnp.ones((1, n), f32)])
    acc[...] = jnp.zeros_like(acc)
    top[...] = jnp.full_like(top, -1e30)

    def step(first, unroll):
        starts = [pl.multiple_of(meta[1 + first + u] * size, size) for u in range(unroll)]
        scores = [
            jnp.dot(key_rows[pl.ds(s, size), :], queries, preferred_element_type=f32)
            for s in starts
        ]
        old = top[...]
        new = old
        for s in scores:
            new = jnp.maximum(new, jnp.max(s, axis=0, keepdims=True))
        total = acc[...] * jnp.exp(old - new)
        for s, start in zip(scores, starts):
            probs = jnp.exp(s - new).astype(bf16)
            total = total + jnp.dot(
                value_cols[:, pl.ds(start, size)], probs, preferred_element_type=f32
            )
        acc[...] = total
        top[...] = new

    block_loops(meta[0], step, long, short)
    exp_total = acc[HD : HD + 1, :]
    out = (acc[:HD, :] / exp_total).astype(bf16)
    for j in range(ot.shape[0]):
        ot[j] = out[:, j * ot.shape[2] : (j + 1) * ot.shape[2]]
    lse[0] = top[...] + jnp.log(exp_total)


def backward_kernel(meta, qt, ot, dot_t, lse, *refs, size, pieces, inner, long, short):
    kv = refs[:pieces]
    dq, keep, send = refs[pieces : pieces + 3]
    key_cols, value_cols, key_rows, query_rows, grad_rows, grad_cols, dq_acc, both = refs[
        pieces + 3 :
    ]
    blocks = pieces * inner
    half = keep.shape[0]
    n = qt.shape[1]
    one = jnp.ones((1, size), f32)
    for e in range(pieces):
        for j in range(inner):
            b = e * inner + j
            here = slice(j * size, (j + 1) * size)
            there = slice(b * size, (b + 1) * size)
            bias = key_bias(meta, b, size, blocks)
            keys = extended(kv[e][:HD, here], [bias, one, one, one])
            key_cols[:, there] = keys
            key_rows[there, :] = keys.T
            value_cols[:, there] = extended(kv[e][HD:, here], [one, one])
    minus = -lse[0]
    high = minus.astype(bf16).astype(f32)
    mid = (minus - high).astype(bf16).astype(f32)
    query_rows[...] = extended(qt[...], [jnp.ones((1, n), f32), high, mid, minus - high - mid]).T
    grads = jnp.concatenate([dot_t[j] for j in range(dot_t.shape[0])], 1)
    outs = jnp.concatenate([ot[j] for j in range(ot.shape[0])], 1)
    grad_cols[...] = grads
    row_dot = -jnp.sum(grads.astype(f32) * outs.astype(f32), axis=0, keepdims=True)
    high = row_dot.astype(bf16).astype(f32)
    grad_rows[...] = extended(grads, [high, row_dot - high]).T
    dq_acc[...] = jnp.zeros_like(dq_acc)
    both[...] = jnp.zeros_like(both)

    def step(first, unroll):
        score_grads, rows, found = [], [], []
        for u in range(unroll):
            b = meta[1 + first + u]
            start = pl.multiple_of(b * size, size)
            probs = jnp.exp(
                jnp.dot(
                    query_rows[...], key_cols[:, pl.ds(start, size)], preferred_element_type=f32
                )
            )
            centred = jnp.dot(
                grad_rows[...], value_cols[:, pl.ds(start, size)], preferred_element_type=f32
            )
            score_grad = (probs * centred).astype(bf16)
            score_grads.append(score_grad)
            rows.append(key_rows[pl.ds(start, size), :])
            dk = jnp.dot(qt[...], score_grad, preferred_element_type=f32)
            dv = jnp.dot(grad_cols[...], probs.astype(bf16), preferred_element_type=f32)
            found.append((b, dk.astype(bf16), dv.astype(bf16)))
        dq_acc[...] += jnp.dot(
            jnp.concatenate(score_grads, 1),
            jnp.concatenate(rows, 0),
            preferred_element_type=f32,
        )
        for b, dk, dv in found:
            lane = pl.multiple_of((b % inner) * size, size)
            both[b // inner, :HD, pl.ds(lane, size)] = dk
            both[b // inner, HD:, pl.ds(lane, size)] = dv

    block_loops(meta[0], step, long, short)
    keep[...] = both[:half]
    send[...] = both[half:]
    dq[...] = (dq_acc[...].T[:HD] * HD ** (-0.5)).astype(bf16)


def unrolled(blocks, most):
    return (most, 2) if blocks % most == 0 else (1, 1)


def attend_forward(meta, qt, kvs, size, first, count):
    n, pieces = qt.shape[1], len(kvs)
    columns = kvs[0].shape[1]
    inner = columns // size
    keys = pieces * columns
    long, short = unrolled(pieces * inner, 8)
    return pl.pallas_call(
        functools.partial(
            forward_kernel, size=size, pieces=pieces, inner=inner, long=long, short=short
        ),
        grid_spec=pltpu.PrefetchScalarGridSpec(
            num_scalar_prefetch=1,
            grid=(count,),
            in_specs=[pl.BlockSpec((HD, n), lambda h, m: (first + h, 0))]
            + [pl.BlockSpec((2 * HD, columns), lambda h, m: (first + h, 0))] * pieces,
            out_specs=[
                pl.BlockSpec((n // size, HD, size), lambda h, m: (0, h, 0)),
                pl.BlockSpec((1, 1, n), lambda h, m: (h, 0, 0)),
            ],
            scratch_shapes=[
                pltpu.VMEM((keys, EXT), bf16),
                pltpu.VMEM((VE, keys), bf16),
                pltpu.VMEM((VE, n), f32),
                pltpu.VMEM((1, n), f32),
            ],
        ),
        out_shape=[
            jax.ShapeDtypeStruct((n // size, count * HD, size), bf16),
            jax.ShapeDtypeStruct((count, 1, n), f32),
        ],
        cost_estimate=pl.CostEstimate(
            flops=20 * count * HD * n * keys,
            bytes_accessed=8 * count * HD * n,
            transcendentals=0,
        ),
        name="attend_forward",
    )(meta, qt, *kvs)


def attend_backward(meta, qt, ot, dot_t, lse, kvs, size, first, count, seq):
    n, pieces = qt.shape[1], len(kvs)
    columns = kvs[0].shape[1]
    inner = columns // size
    keys = pieces * columns
    half = (pieces + 1) // 2
    long, short = unrolled(pieces * inner, 4)
    row_spec = pl.BlockSpec((HD, n), lambda h, m: (first + h, 0))
    split_spec = pl.BlockSpec((n // size, HD, size), lambda h, m: (0, first + h, 0))
    grad_spec = pl.BlockSpec((n // size, HD, size), lambda h, m: (0, first + h, seq))
    part_spec = pl.BlockSpec((half, 2 * HD, columns), lambda h, m: (0, h, 0))
    part_shape = jax.ShapeDtypeStruct((half, 2 * HD * count, columns), bf16)
    return pl.pallas_call(
        functools.partial(
            backward_kernel, size=size, pieces=pieces, inner=inner, long=long, short=short
        ),
        grid_spec=pltpu.PrefetchScalarGridSpec(
            num_scalar_prefetch=1,
            grid=(count,),
            in_specs=[row_spec, split_spec, grad_spec]
            + [pl.BlockSpec((1, 1, n), lambda h, m: (first + h, 0, 0))]
            + [pl.BlockSpec((2 * HD, columns), lambda h, m: (first + h, 0))] * pieces,
            out_specs=[pl.BlockSpec((HD, n), lambda h, m: (h, 0)), part_spec, part_spec],
            scratch_shapes=[
                pltpu.VMEM((EXT, keys), bf16),
                pltpu.VMEM((EXT, keys), bf16),
                pltpu.VMEM((keys, EXT), bf16),
                pltpu.VMEM((n, EXT), bf16),
                pltpu.VMEM((n, EXT), bf16),
                pltpu.VMEM((HD, n), bf16),
                pltpu.VMEM((n, EXT), f32),
                pltpu.VMEM((pieces, 2 * HD, columns), bf16),
            ],
        ),
        out_shape=[jax.ShapeDtypeStruct((count * HD, n), bf16), part_shape, part_shape],
        cost_estimate=pl.CostEstimate(
            flops=count * HD * n,
            bytes_accessed=count * HD * n,
            transcendentals=0,
        ),
        name="attend_backward",
    )(meta, qt, ot, dot_t, lse, *kvs)


def weight_grad_kernel(
    pre, hidden, act, grad, mixed_t, mixer, vectors, out, mixed_sum, *, tp_n, step, tail
):
    half, piece = pl.program_id(0), pl.program_id(1)

    @pl.when((half == 0) & (piece == 0))
    def _():
        mixed_sum[...] = jnp.dot(mixed_t[...], mixer[...], preferred_element_type=f32)

    quarter = pre.shape[1] // tp_n

    def fill(left, right):
        found = lax.dot_general(
            left, right, (((0,), (0,)), ((), ())), preferred_element_type=f32
        ).astype(bf16)
        for t in range(tp_n):
            out[0, t * step : t * step + quarter, :] = found[t * quarter : (t + 1) * quarter]

    @pl.when(half == 0)
    def _():
        fill(pre[...], hidden[...])

    @pl.when(half == 1)
    def _():
        fill(act[...], grad[...])

    width = mixed_sum.shape[0] // tp_n
    for t in range(tp_n):
        start = pl.multiple_of(t * width + (piece * 2 + half) * tail, 8)
        ending = jnp.concatenate([mixed_sum[pl.ds(start, tail), :], vectors[half]], 0)
        out[0, t * step + quarter : (t + 1) * step, :] = ending.astype(bf16)


def weight_grads(pre, hidden, act, grad, mixed_t, mixer, vectors, pieces, tp_n, step, tail):
    n, columns = pre.shape
    width = hidden.shape[1]
    tile = columns // pieces
    whole = lambda x: pl.BlockSpec(x.shape, lambda g, i: (0, 0))
    return pl.pallas_call(
        functools.partial(weight_grad_kernel, tp_n=tp_n, step=step, tail=tail),
        grid=(2, pieces),
        in_specs=[
            pl.BlockSpec((n, tile), lambda g, i: (0, i * (1 - g) + (pieces - 1) * g)),
            whole(hidden),
            pl.BlockSpec((n, tile), lambda g, i: (0, i * g)),
            whole(grad),
            whole(mixed_t),
            whole(mixer),
            pl.BlockSpec(vectors.shape, lambda g, i: (0, 0, 0)),
        ],
        out_specs=pl.BlockSpec((1, tp_n * step, width), lambda g, i: (g, i, 0)),
        out_shape=jax.ShapeDtypeStruct((2, pieces * tp_n * step, width), bf16),
        scratch_shapes=[pltpu.VMEM((mixed_t.shape[0], width), f32)],
        cost_estimate=pl.CostEstimate(
            flops=4 * n * columns * width, bytes_accessed=8 * n * columns, transcendentals=0
        ),
        name="weight_grads",
    )(pre, hidden, act, grad, mixed_t, mixer, vectors)


def swap(x, axis, bits):
    return lax.ppermute(x, axis, [(i, i ^ bits) for i in range(lax.axis_size(axis))])


def wide(x):
    return x.astype(f32)


def low(x):
    return x.astype(bf16)


def dot(a, b, contract):
    return lax.dot_general(a, b, (contract, ((), ())), preferred_element_type=f32)


NN = ((1,), (0,))
NT = ((1,), (1,))
TN = ((0,), (0,))


def xor_order(x, axis, index):
    n = x.shape[axis]
    bit = 1
    while bit < n:
        moved = jnp.stack([lax.index_in_dim(x, i ^ bit, axis, False) for i in range(n)], axis)
        x = jnp.where((index & bit) != 0, moved, x)
        bit *= 2
    return x


def norm_forward(resid, gain, shift):
    centre = resid - jnp.mean(resid, axis=-1, keepdims=True)
    factor = lax.rsqrt(jnp.mean(centre * centre, axis=-1, keepdims=True) + epsilon)
    normed = centre * factor
    return (normed * gain + shift, normed, factor)


def norm_backward(grad_out, normed, factor, gain):
    scaled = grad_out * gain
    centred = scaled - jnp.mean(scaled, axis=-1, keepdims=True)
    return factor * (centred - normed * jnp.mean(scaled * normed, axis=-1, keepdims=True))


def on_device(
    tokens,
    cotangent,
    lengths,
    query_weight,
    query_bias,
    key_weight,
    value_weight,
    value_bias,
    out_weight,
    out_bias,
    first_gain,
    first_shift,
    up_weight,
    up_bias,
    down_weight,
    down_bias,
    second_gain,
    second_shift,
):
    shard_n, ctx_n, tp_n = (lax.axis_size(a) for a in ("shard", "ctx", "tp"))
    shard_i, ctx_i, tp_i = (lax.axis_index(a) for a in ("shard", "ctx", "tp"))
    seqs, rows, model = tokens.shape
    part = model // shard_n
    width = query_weight.shape[1]
    heads = width // HD
    units = up_weight.shape[1]
    quarter = units // ctx_n
    two = shard_n == 2
    first = shard_i == 0

    def flip(x):
        if not two:
            return x
        return jnp.where(first, x, jnp.concatenate([x[..., part:], x[..., :part]], -1))

    def gather_local(x):
        if two:
            return jnp.concatenate([x, swap(x, "shard", 1)], -1)
        return lax.all_gather(x, "shard", axis=x.ndim - 1, tiled=True)

    def scatter_local(x):
        if two:
            return wide(x[:, :part]) + wide(swap(x[:, part:], "shard", 1))
        return wide(lax.psum_scatter(x, "shard", scatter_dimension=1, tiled=True))

    def after(x, *gates):
        return lax.optimization_barrier((x, *gates))[0]

    bits = ctx_n.bit_length() - 1
    ctx_bits = [1 << i for i in reversed(range(bits))]

    def bit_reverse(e):
        return sum(((e >> i) & 1) << (bits - 1 - i) for i in range(bits))

    ctx_order = [bit_reverse(e) for e in range(ctx_n)]
    half = (ctx_n + 1) // 2

    def exchange(x):
        return lax.all_to_all(x, "tp", 0, 0, tiled=True)

    def tp_gather(x):
        return exchange(jnp.broadcast_to(x[None], (tp_n, *x.shape)))

    def ctx_gather(chunks, some=None):
        for bit in ctx_bits if some is None else some:
            chunks = chunks + [swap(c, "ctx", bit) for c in chunks]
        return chunks

    kv_t = jnp.stack(
        [key_weight.T.reshape(heads, HD, part), value_weight.T.reshape(heads, HD, part)], 1
    ).reshape(2 * width, part)
    mine = lambda w: lax.dynamic_slice_in_dim(w, ctx_i * quarter, quarter, 0)
    qkv_t = flip(gather_local(jnp.concatenate([query_weight.T, kv_t], 0)))
    kv_bias = jnp.stack(
        [jnp.zeros((heads, HD), f32), value_bias.reshape(heads, HD)], 1
    ).reshape(2 * width, 1)

    first_in = tp_gather(tokens[0])
    blocks = [first_in.reshape(tp_n * rows, model)]
    for s in range(1, seqs):
        blocks.append(tp_gather(after(tokens[s], blocks[-1])).reshape(tp_n * rows, model))

    bias_rows = []
    rest = up_bias
    for _ in range(3):
        bias_rows.append(low(rest))
        rest = rest - wide(bias_rows[-1])
    extra = 3 * units // model
    bias_rows = jnp.stack(bias_rows, 0).reshape(extra, model)
    bias_rows = lax.dynamic_slice_in_dim(bias_rows, shard_i * part, part, 1)
    tail = width // ctx_n // 2
    step = -(-(quarter + tail + extra) // 16) * 16
    out_mine = lax.dynamic_slice_in_dim(out_weight, ctx_i * 2 * tail, 2 * tail, 0)
    fill = jnp.zeros((step - quarter - tail - extra, part), bf16)
    pack = jnp.stack(
        [
            jnp.concatenate([mine(up_weight.T), bias_rows, fill, out_mine[:tail]], 0),
            jnp.concatenate(
                [mine(down_weight), jnp.zeros((extra, part), bf16), fill, out_mine[tail:]], 0
            ),
        ],
        0,
    )
    pack = lax.all_gather(after(pack, blocks[-1]), "tp", axis=1, tiled=True)
    chunk = tp_n * step
    ups = [gather_local(pack[0])]
    downs = after(jnp.concatenate(ctx_gather([pack[1]], ctx_bits[:-1]), 0), *ups)

    place = jnp.arange(ctx_n * tp_n)
    order = bit_reverse((place // tp_n) ^ ctx_i) * tp_n + place % tp_n
    block_at = (bit_reverse(place // tp_n) ^ ctx_i) * tp_n + place % tp_n

    def project(s, block):
        kv = low(dot(qkv_t[width:], block, NT) + kv_bias)
        q = low(dot(qkv_t[:width], block, NT) + query_bias[:, None])
        return kv, q * bf16(HD ** (-0.5))

    def ctx_pieces(kv, gate):
        chunks = [kv]
        for bit in ctx_bits:
            chunks = chunks + [swap(c, "ctx", bit) for c in chunks]
            if gate is not None and bit == ctx_bits[0]:
                chunks = [after(c, gate) for c in chunks]
        return chunks

    metas = []
    for s in range(seqs):
        count = jnp.clip(lengths[s] - block_at * rows, 0, rows)
        metas.append(
            jnp.concatenate([((lengths[s] + rows - 1) // rows)[None], order, count]).astype(
                jnp.int32
            )
        )

    outs, totals, attended, queries, keys_values = [], [], [], [], []
    kv, q = project(0, blocks[0])
    kvs = ctx_pieces(kv, None)
    for s in range(seqs):
        keys_values.append(kvs)
        queries.append(q)
        if s + 1 < seqs and heads > 1:
            ot_a, lse_a = attend_forward(metas[s], q, kvs, rows, 0, heads - 1)
            kv_next, q_next = project(s + 1, after(blocks[s + 1], lse_a))
            meta = after(metas[s], kv_next, q_next)
            ot_b, lse_b = attend_forward(meta, q, kvs, rows, heads - 1, 1)
            ot = jnp.concatenate([ot_a, ot_b], 1)
            lse = jnp.concatenate([lse_a, lse_b], 0)
            q, kvs = q_next, ctx_pieces(kv_next, lse_b)
        else:
            ot_a, lse_a = attend_forward(metas[s], q, kvs, rows, 0, heads - 1)
            meta = after(metas[s], lse_a, ups[0], downs)
            ot_b, lse_b = attend_forward(meta, q, kvs, rows, heads - 1, 1)
            ot = jnp.concatenate([ot_a, ot_b], 1)
            lse = jnp.concatenate([lse_a, lse_b], 0)
        outs.append(ot)
        totals.append(lse)
        attended.append(exchange(ot).reshape(tp_n * width, rows))
    ups = ctx_gather(ups)
    downs = after(gather_local(downs), attended[-1])
    downs = [downs[i * chunk : (i + 1) * chunk] for i in range(half)]
    downs = ctx_gather(downs, ctx_bits[-1:])

    def natural(pieces):
        whole = jnp.zeros((ctx_n, *pieces[0].shape), bf16)
        for e, piece in zip(ctx_order, pieces):
            whole = lax.dynamic_update_slice_in_dim(whole, piece[None], e ^ ctx_i, 0)
        return whole

    ups = [x.reshape(tp_n, step, model) for x in ups]
    downs = [x.reshape(tp_n, step, model) for x in downs]
    up_full = natural([x[:, :quarter] for x in ups]).reshape(-1, model)
    down_full = natural([x[:, :quarter] for x in downs]).reshape(-1, model)
    ends = [
        jnp.stack([x[:, step - tail :] for x in pair], 1) for pair in zip(ups, downs)
    ]
    out_full = natural(ends).transpose(1, 0, 2, 3, 4).reshape(tp_n * width, model)
    unit_bias = wide(flip(ups[0][:, quarter : quarter + extra]))
    unit_bias = unit_bias.reshape(tp_n, 3, ctx_n, quarter)
    unit_bias = (unit_bias[:, 0] + unit_bias[:, 1]) + unit_bias[:, 2]
    unit_bias = unit_bias.transpose(1, 0, 2).reshape(1, ctx_n * tp_n * quarter)

    attended_t = jnp.concatenate(attended, 1)

    flat = flip(wide(tokens.reshape(seqs * rows, model)))
    cot = flip(wide(cotangent.reshape(seqs * rows, model)))
    gain_1, shift_1, gain_2, shift_2, bias_o, bias_d = (
        flip(v) for v in (first_gain, first_shift, second_gain, second_shift, out_bias, down_bias)
    )
    mixed = dot(attended_t, out_full, TN) + bias_o
    hidden, normed_1, factor_1 = norm_forward(flat + mixed, gain_1, shift_1)
    hidden_low = low(hidden)
    pre = dot(hidden_low, up_full, NT) + unit_bias
    share = 0.5 * (1.0 + lax.erf(pre * 0.5**0.5))
    activated = low(pre * share)
    slope = low(share + pre * jnp.exp(-0.5 * pre * pre) * 0.3989422804014327)
    ffn_out = dot(activated, down_full, NN) + bias_d
    result, normed_2, factor_2 = norm_forward(hidden + ffn_out, gain_2, shift_2)
    here = (ctx_i * tp_n + tp_i) * rows + jnp.arange(rows)
    valid = (here[None, :] < lengths[:, None]).reshape(seqs * rows, 1)
    grad_result = jnp.where(valid, cot, 0.0)
    gain_2_grad = jnp.sum(grad_result * normed_2, axis=0)
    shift_2_grad = jnp.sum(grad_result, axis=0)
    grad_second = norm_backward(grad_result, normed_2, factor_2, gain_2)
    ffn_grad = low(grad_second)
    bias_d_grad = jnp.sum(wide(ffn_grad), axis=0)
    pre_grad = low(dot(ffn_grad, down_full, NT) * wide(slope))
    grad_hidden = grad_second + dot(pre_grad, up_full, NN)
    up_bias_grad = jnp.sum(wide(pre_grad), axis=0)
    gain_1_grad = jnp.sum(grad_hidden * normed_1, axis=0)
    shift_1_grad = jnp.sum(grad_hidden, axis=0)
    grad_first = norm_backward(grad_hidden, normed_1, factor_1, gain_1)
    mixer_grad = low(grad_first)
    bias_o_grad = jnp.sum(wide(mixer_grad), axis=0)
    attended_grad_t = low(dot(out_full, mixer_grad, NT))
    value_bias_parts = jnp.sum(
        wide(attended_grad_t).reshape(tp_n, width, seqs * rows), axis=2
    )
    value_bias_grad = value_bias_parts.reshape(-1)
    up_bias_full = up_bias_grad.reshape(ctx_n, tp_n, quarter).transpose(1, 0, 2).reshape(-1)
    up_rows = up_bias_full.shape[0] // model
    vectors = [
        flip(value_bias_grad),
        bias_o_grad,
        gain_1_grad,
        shift_1_grad,
        flip(up_bias_full.reshape(up_rows, model)),
        bias_d_grad,
        gain_2_grad,
        shift_2_grad,
    ]
    vectors = [p for v in vectors for p in v.reshape(-1, model)]
    grad_step = -(-(quarter + tail + (len(vectors) + 1) // 2) // 16) * 16
    spare = grad_step - quarter - tail
    vectors = sum(
        jnp.pad(v[None], ((i, 2 * spare - 1 - i), (0, 0))) for i, v in enumerate(vectors)
    ).reshape(2, spare, model)

    grad_cols = exchange(attended_grad_t.reshape(tp_n, width, seqs * rows))

    def sum_ctx(x):
        for bit in reversed(ctx_bits):
            x = low(x)
            x = wide(x) + wide(swap(x, "ctx", bit))
        return x

    late_pre = after(pre_grad, attended_grad_t)
    ffn_grads = weight_grads(
        late_pre,
        hidden_low,
        activated,
        ffn_grad,
        attended_t,
        mixer_grad,
        vectors,
        ctx_n,
        tp_n,
        grad_step,
        tail,
    )
    ffn_sum = lax.psum_scatter(
        after(ffn_grads, grad_cols), ("ctx", "tp"), scatter_dimension=1, tiled=True
    )

    grad_rows = flip(grad_first).reshape(seqs, rows, model)
    spans = []
    for s in range(seqs):
        if s + 1 < seqs or heads == 1:
            spans.append((s, 0, heads))
        else:
            spans += [(s, 0, 1), (s, 1, heads - 1)]
    near = ctx_bits[-1:]
    far = list(reversed(ctx_bits[:-1]))

    def near_sum(keep, send):
        got = send
        for bit in near:
            got = swap(send, "ctx", bit)
        return [(keep[p], got[p]) if p == 0 else low(wide(keep[p]) + wide(got[p])) for p in range(half)]

    def far_sum(chunks):
        first, rest = chunks[0], chunks[1:]
        total = wide(first[0]) + wide(first[1])
        if len(far) == 1:
            return low(total + wide(swap(rest[0], "ctx", far[0])))
        chunks = [low(total)] + rest
        for bit in far:
            n = len(chunks) // 2
            chunks = [
                low(wide(a) + wide(swap(b, "ctx", bit))) for a, b in zip(chunks[:n], chunks[n:])
            ]
        return chunks[0]

    qkv_grad = 0.0
    sums = 0.0
    dq_parts = [[] for _ in range(seqs)]
    dkv_parts = [[] for _ in range(seqs)]
    last = ()
    near_chunks = None
    number = 0

    def finish(s, *gates):
        grads_t = jnp.concatenate(dq_parts[s] + dkv_parts[s], 0)
        back = low(dot(grads_t, qkv_t, TN))
        if gates:
            back = after(back, *gates)
        cut = back.reshape(tp_n, rows, model)
        if s + 1 < seqs:
            total = [lax.dynamic_index_in_dim(cut, tp_i, 0, False)] + [
                swap(lax.dynamic_index_in_dim(cut, tp_i ^ j, 0, False), "tp", j)
                for j in range(1, tp_n)
            ]
        else:
            total = [lax.psum_scatter(back, "tp", scatter_dimension=0, tiled=True)]
        return (
            back,
            total,
            dot(after(grads_t, back), blocks[s], NN),
            jnp.sum(wide(jnp.concatenate(dq_parts[s], 0)), axis=1),
        )

    def received(s, parts):
        total = grad_rows[s]
        for p in parts:
            total = total + wide(p)
        return low(total)

    moving = {}
    for s, start, count in spans:
        meta = metas[s]
        wait = list(last) if last else [grad_cols]
        if number >= 1:
            wait += near_chunks[1:]
        if number >= 2:
            done_s = spans[number - 2][0]
            wait.append(dkv_parts[done_s][-1])
            if spans[number - 1][0] != done_s:
                done = finish(done_s)
                wait.append(done[0])
                moving[done_s] = done[1]
                qkv_grad, sums = qkv_grad + done[2], sums + done[3]
        if wait:
            meta = after(meta, *wait)
        dq, keep, send = attend_backward(
            meta, queries[s], outs[s], grad_cols, totals[s], keys_values[s], rows, start, count, s
        )
        last = (dq,)
        number += 1
        if number > 1:
            before = spans[number - 2][0]
            keep, send, dkv_parts[before][-1] = lax.optimization_barrier(
                (keep, send, dkv_parts[before][-1])
            )
            for parts in moving.values():
                keep, send, parts[1:] = lax.optimization_barrier((keep, send, parts[1:]))
        near_chunks = near_sum(keep, send)
        dq_parts[s].append(dq)
        dkv_parts[s].append(far_sum(near_chunks))
    ffn_sum = low(scatter_local(ffn_sum.reshape(2 * grad_step, model)))
    done = finish(seqs - 1)
    moving[seqs - 1] = done[1]
    qkv_grad, sums = qkv_grad + done[2], sums + done[3]
    chunks = ctx_gather([ffn_sum])
    stacked = jnp.stack([chunks[ctx_order.index(e)] for e in range(ctx_n)], 0)
    stacked = xor_order(stacked, 0, ctx_i).reshape(ctx_n, 2, grad_step, part)
    summed = stacked[0, :, quarter + tail :].reshape(2 * spare, part)
    for i in range(tp_n.bit_length() - 1):
        summed = jnp.where((tp_i >> i) & 1 != 0, swap(summed, "tp", 1 << i), summed)
    summed = wide(flip(gather_local(summed)))
    stacked = wide(stacked)
    up_sum = stacked[:, 0, :quarter].reshape(units, part)
    down_sum = stacked[:, 1, :quarter].reshape(units, part)
    out_sum = stacked[:, :, quarter : quarter + tail].reshape(width, part)

    if two:
        sums = jnp.pad(sums, (0, part - width))
        sums = jnp.pad(jnp.concatenate([sums, sums])[None], ((0, 15), (0, 0)))
        qkv_sum = scatter_local(flip(low(jnp.concatenate([qkv_grad, sums], 0))))
        qkv_sum = sum_ctx(qkv_sum)
        query_bias_sum = qkv_sum[3 * width, :width]
    else:
        qkv_sum = sum_ctx(scatter_local(low(qkv_grad)))
        query_bias_sum = lax.psum(sums, ("shard", "ctx"))
    query_sum = qkv_sum[:width]
    kv_sum = qkv_sum[width : 3 * width].reshape(heads, 2, HD, part)
    key_sum = kv_sum[:, 0].reshape(width, part)
    value_sum = kv_sum[:, 1].reshape(width, part)

    query_bias_parts = [query_bias_sum] + [swap(query_bias_sum, "tp", j) for j in range(1, tp_n)]
    query_bias_full = xor_order(jnp.stack(query_bias_parts, 0), 0, tp_i).reshape(-1)
    moving[seqs - 1][0] = after(moving[seqs - 1][0], query_bias_full, out_sum)
    input_grads = jnp.stack([received(s, moving[s]) for s in range(seqs)], 0)
    ends = [*summed[:4], summed[4 : 4 + up_rows].reshape(-1), *summed[4 + up_rows : 7 + up_rows]]
    return (
        low(flip(result)).reshape(seqs, rows, model),
        input_grads,
        query_sum.T,
        query_bias_full,
        key_sum.T,
        value_sum.T,
        ends[0],
        out_sum,
        ends[1],
        ends[2],
        ends[3],
        up_sum.T,
        ends[4],
        down_sum,
        ends[5],
        ends[6],
        ends[7],
    )


def solution(mesh):
    placed = (
        P("shard", ("ctx", "tp"), None),
        P("shard", ("ctx", "tp"), None),
        P("shard"),
        P("shard", "tp"),
        P("tp"),
        P("shard", "tp"),
        P("shard", "tp"),
        P("tp"),
        P("tp", "shard"),
        P(),
        P(),
        P(),
        P("shard", "tp"),
        P("tp"),
        P("tp", "shard"),
        P(),
        P(),
        P(),
    )
    return jax.shard_map(
        on_device,
        mesh=mesh,
        in_specs=placed,
        out_specs=(
            P("shard", ("ctx", "tp"), None),
            P("shard", ("ctx", "tp"), None),
            P("shard", "tp"),
            P(),
            P("shard", "tp"),
            P("shard", "tp"),
            P(),
            P("tp", "shard"),
            P(),
            P(),
            P(),
            P("shard", "tp"),
            P(),
            P("tp", "shard"),
            P(),
            P(),
            P(),
        ),
        check_vma=False,
    )
```

```python
import functools

import jax
import jax.numpy as jnp
from jax import lax
from jax.experimental import pallas as pl
from jax.experimental.pallas import tpu as pltpu
from jax.sharding import PartitionSpec as P

HD = 64
EXT = 128
VE = 80
epsilon = 1e-12
f32 = jnp.float32
bf16 = jnp.bfloat16


def extended(block, extra_rows):
    n = block.shape[1]
    row = lax.broadcasted_iota(jnp.int32, (EXT - HD, n), 0)
    extra = jnp.zeros((EXT - HD, n), f32)
    for place, values in enumerate(extra_rows):
        extra = jnp.where(row == place, values, extra)
    return jnp.concatenate([block, extra.astype(bf16)], axis=0)


def key_bias(meta, block, size, blocks):
    count = meta[1 + blocks + block]
    lane = lax.broadcasted_iota(jnp.int32, (1, size), 1)
    return jnp.where(lane < count, 0.0, -1e30).astype(f32)


def block_loops(count, step, long, short):
    def long_step(i, carry):
        step(i * long, long)
        return carry

    def short_step(i, carry):
        step(whole * long + i * short, short)
        return carry

    whole = count // long
    lax.fori_loop(0, whole, long_step, 0)
    lax.fori_loop(0, (count - whole * long + short - 1) // short, short_step, 0)


def forward_kernel(meta, qt, *refs, size, pieces, inner, long, short):
    kv = refs[:pieces]
    ot, lse, key_rows, value_cols, acc, top = refs[pieces:]
    blocks = pieces * inner
    n = qt.shape[1]
    one = jnp.ones((1, size), f32)
    for e in range(pieces):
        for j in range(inner):
            b = e * inner + j
            here = slice(j * size, (j + 1) * size)
            there = slice(b * size, (b + 1) * size)
            bias = key_bias(meta, b, size, blocks)
            key_rows[there, :] = extended(kv[e][:HD, here], [bias]).T
            value_cols[:, there] = extended(kv[e][HD:, here], [one])[:VE]
    queries = extended(qt[...], [jnp.ones((1, n), f32)])
    acc[...] = jnp.zeros_like(acc)
    top[...] = jnp.full_like(top, -1e30)

    def step(first, unroll):
        starts = [pl.multiple_of(meta[1 + first + u] * size, size) for u in range(unroll)]
        scores = [
            jnp.dot(key_rows[pl.ds(s, size), :], queries, preferred_element_type=f32)
            for s in starts
        ]
        old = top[...]
        new = old
        for s in scores:
            new = jnp.maximum(new, jnp.max(s, axis=0, keepdims=True))
        total = acc[...] * jnp.exp(old - new)
        for s, start in zip(scores, starts):
            probs = jnp.exp(s - new).astype(bf16)
            total = total + jnp.dot(
                value_cols[:, pl.ds(start, size)], probs, preferred_element_type=f32
            )
        acc[...] = total
        top[...] = new

    block_loops(meta[0], step, long, short)
    exp_total = acc[HD : HD + 1, :]
    out = (acc[:HD, :] / exp_total).astype(bf16)
    for j in range(ot.shape[0]):
        ot[j] = out[:, j * ot.shape[2] : (j + 1) * ot.shape[2]]
    lse[0] = top[...] + jnp.log(exp_total)


def backward_kernel(meta, qt, ot, dot_t, lse, *refs, size, pieces, inner, long, short):
    kv = refs[:pieces]
    dq, keep, send = refs[pieces : pieces + 3]
    key_cols, value_cols, key_rows, query_rows, grad_rows, grad_cols, dq_acc, both = refs[
        pieces + 3 :
    ]
    blocks = pieces * inner
    half = keep.shape[0]
    n = qt.shape[1]
    one = jnp.ones((1, size), f32)
    for e in range(pieces):
        for j in range(inner):
            b = e * inner + j
            here = slice(j * size, (j + 1) * size)
            there = slice(b * size, (b + 1) * size)
            bias = key_bias(meta, b, size, blocks)
            keys = extended(kv[e][:HD, here], [bias, one, one, one])
            key_cols[:, there] = keys
            key_rows[there, :] = keys.T
            value_cols[:, there] = extended(kv[e][HD:, here], [one, one])
    minus = -lse[0]
    high = minus.astype(bf16).astype(f32)
    mid = (minus - high).astype(bf16).astype(f32)
    query_rows[...] = extended(qt[...], [jnp.ones((1, n), f32), high, mid, minus - high - mid]).T
    grads = jnp.concatenate([dot_t[j] for j in range(dot_t.shape[0])], 1)
    outs = jnp.concatenate([ot[j] for j in range(ot.shape[0])], 1)
    grad_cols[...] = grads
    row_dot = -jnp.sum(grads.astype(f32) * outs.astype(f32), axis=0, keepdims=True)
    high = row_dot.astype(bf16).astype(f32)
    grad_rows[...] = extended(grads, [high, row_dot - high]).T
    dq_acc[...] = jnp.zeros_like(dq_acc)
    both[...] = jnp.zeros_like(both)

    def step(first, unroll):
        score_grads, rows, found = [], [], []
        for u in range(unroll):
            b = meta[1 + first + u]
            start = pl.multiple_of(b * size, size)
            probs = jnp.exp(
                jnp.dot(
                    query_rows[...], key_cols[:, pl.ds(start, size)], preferred_element_type=f32
                )
            )
            centred = jnp.dot(
                grad_rows[...], value_cols[:, pl.ds(start, size)], preferred_element_type=f32
            )
            score_grad = (probs * centred).astype(bf16)
            score_grads.append(score_grad)
            rows.append(key_rows[pl.ds(start, size), :])
            dk = jnp.dot(qt[...], score_grad, preferred_element_type=f32)
            dv = jnp.dot(grad_cols[...], probs.astype(bf16), preferred_element_type=f32)
            found.append((b, dk.astype(bf16), dv.astype(bf16)))
        dq_acc[...] += jnp.dot(
            jnp.concatenate(score_grads, 1),
            jnp.concatenate(rows, 0),
            preferred_element_type=f32,
        )
        for b, dk, dv in found:
            lane = pl.multiple_of((b % inner) * size, size)
            both[b // inner, :HD, pl.ds(lane, size)] = dk
            both[b // inner, HD:, pl.ds(lane, size)] = dv

    block_loops(meta[0], step, long, short)
    keep[...] = both[:half]
    send[...] = both[half:]
    dq[...] = (dq_acc[...].T[:HD] * HD ** (-0.5)).astype(bf16)


def unrolled(blocks, most):
    return (most, 2) if blocks % most == 0 else (1, 1)


def attend_forward(meta, qt, kvs, size, first, count):
    n, pieces = qt.shape[1], len(kvs)
    columns = kvs[0].shape[1]
    inner = columns // size
    keys = pieces * columns
    long, short = unrolled(pieces * inner, 8)
    return pl.pallas_call(
        functools.partial(
            forward_kernel, size=size, pieces=pieces, inner=inner, long=long, short=short
        ),
        grid_spec=pltpu.PrefetchScalarGridSpec(
            num_scalar_prefetch=1,
            grid=(count,),
            in_specs=[pl.BlockSpec((HD, n), lambda h, m: (first + h, 0))]
            + [pl.BlockSpec((2 * HD, columns), lambda h, m: (first + h, 0))] * pieces,
            out_specs=[
                pl.BlockSpec((n // size, HD, size), lambda h, m: (0, h, 0)),
                pl.BlockSpec((1, 1, n), lambda h, m: (h, 0, 0)),
            ],
            scratch_shapes=[
                pltpu.VMEM((keys, EXT), bf16),
                pltpu.VMEM((VE, keys), bf16),
                pltpu.VMEM((VE, n), f32),
                pltpu.VMEM((1, n), f32),
            ],
        ),
        out_shape=[
            jax.ShapeDtypeStruct((n // size, count * HD, size), bf16),
            jax.ShapeDtypeStruct((count, 1, n), f32),
        ],
        cost_estimate=pl.CostEstimate(
            flops=20 * count * HD * n * keys,
            bytes_accessed=8 * count * HD * n,
            transcendentals=0,
        ),
        name="attend_forward",
    )(meta, qt, *kvs)


def attend_backward(meta, qt, ot, dot_t, lse, kvs, size, first, count, seq):
    n, pieces = qt.shape[1], len(kvs)
    columns = kvs[0].shape[1]
    inner = columns // size
    keys = pieces * columns
    half = (pieces + 1) // 2
    long, short = unrolled(pieces * inner, 4)
    row_spec = pl.BlockSpec((HD, n), lambda h, m: (first + h, 0))
    split_spec = pl.BlockSpec((n // size, HD, size), lambda h, m: (0, first + h, 0))
    grad_spec = pl.BlockSpec((n // size, HD, size), lambda h, m: (0, first + h, seq))
    part_spec = pl.BlockSpec((half, 2 * HD, columns), lambda h, m: (0, h, 0))
    part_shape = jax.ShapeDtypeStruct((half, 2 * HD * count, columns), bf16)
    return pl.pallas_call(
        functools.partial(
            backward_kernel, size=size, pieces=pieces, inner=inner, long=long, short=short
        ),
        grid_spec=pltpu.PrefetchScalarGridSpec(
            num_scalar_prefetch=1,
            grid=(count,),
            in_specs=[row_spec, split_spec, grad_spec]
            + [pl.BlockSpec((1, 1, n), lambda h, m: (first + h, 0, 0))]
            + [pl.BlockSpec((2 * HD, columns), lambda h, m: (first + h, 0))] * pieces,
            out_specs=[pl.BlockSpec((HD, n), lambda h, m: (h, 0)), part_spec, part_spec],
            scratch_shapes=[
                pltpu.VMEM((EXT, keys), bf16),
                pltpu.VMEM((EXT, keys), bf16),
                pltpu.VMEM((keys, EXT), bf16),
                pltpu.VMEM((n, EXT), bf16),
                pltpu.VMEM((n, EXT), bf16),
                pltpu.VMEM((HD, n), bf16),
                pltpu.VMEM((n, EXT), f32),
                pltpu.VMEM((pieces, 2 * HD, columns), bf16),
            ],
        ),
        out_shape=[jax.ShapeDtypeStruct((count * HD, n), bf16), part_shape, part_shape],
        cost_estimate=pl.CostEstimate(
            flops=count * HD * n,
            bytes_accessed=count * HD * n,
            transcendentals=0,
        ),
        name="attend_backward",
    )(meta, qt, ot, dot_t, lse, *kvs)


def weight_grad_kernel(
    pre, hidden, act, grad, mixed_t, mixer, vectors, out, mixed_sum, *, tp_n, step, tail
):
    half, piece = pl.program_id(0), pl.program_id(1)

    @pl.when((half == 0) & (piece == 0))
    def _():
        mixed_sum[...] = jnp.dot(mixed_t[...], mixer[...], preferred_element_type=f32)

    quarter = pre.shape[1] // tp_n

    def fill(left, right):
        found = lax.dot_general(
            left, right, (((0,), (0,)), ((), ())), preferred_element_type=f32
        ).astype(bf16)
        for t in range(tp_n):
            out[0, t * step : t * step + quarter, :] = found[t * quarter : (t + 1) * quarter]

    @pl.when(half == 0)
    def _():
        fill(pre[...], hidden[...])

    @pl.when(half == 1)
    def _():
        fill(act[...], grad[...])

    width = mixed_sum.shape[0] // tp_n
    for t in range(tp_n):
        start = pl.multiple_of(t * width + (piece * 2 + half) * tail, 8)
        ending = jnp.concatenate([mixed_sum[pl.ds(start, tail), :], vectors[half]], 0)
        out[0, t * step + quarter : (t + 1) * step, :] = ending.astype(bf16)


def weight_grads(pre, hidden, act, grad, mixed_t, mixer, vectors, pieces, tp_n, step, tail):
    n, columns = pre.shape
    width = hidden.shape[1]
    tile = columns // pieces
    whole = lambda x: pl.BlockSpec(x.shape, lambda g, i: (0, 0))
    return pl.pallas_call(
        functools.partial(weight_grad_kernel, tp_n=tp_n, step=step, tail=tail),
        grid=(2, pieces),
        in_specs=[
            pl.BlockSpec((n, tile), lambda g, i: (0, i * (1 - g) + (pieces - 1) * g)),
            whole(hidden),
            pl.BlockSpec((n, tile), lambda g, i: (0, i * g)),
            whole(grad),
            whole(mixed_t),
            whole(mixer),
            pl.BlockSpec(vectors.shape, lambda g, i: (0, 0, 0)),
        ],
        out_specs=pl.BlockSpec((1, tp_n * step, width), lambda g, i: (g, i, 0)),
        out_shape=jax.ShapeDtypeStruct((2, pieces * tp_n * step, width), bf16),
        scratch_shapes=[pltpu.VMEM((mixed_t.shape[0], width), f32)],
        cost_estimate=pl.CostEstimate(
            flops=4 * n * columns * width, bytes_accessed=8 * n * columns, transcendentals=0
        ),
        name="weight_grads",
    )(pre, hidden, act, grad, mixed_t, mixer, vectors)


def swap(x, axis, bits):
    return lax.ppermute(x, axis, [(i, i ^ bits) for i in range(lax.axis_size(axis))])


def wide(x):
    return x.astype(f32)


def low(x):
    return x.astype(bf16)


def dot(a, b, contract):
    return lax.dot_general(a, b, (contract, ((), ())), preferred_element_type=f32)


NN = ((1,), (0,))
NT = ((1,), (1,))
TN = ((0,), (0,))


def xor_order(x, axis, index):
    n = x.shape[axis]
    bit = 1
    while bit < n:
        moved = jnp.stack([lax.index_in_dim(x, i ^ bit, axis, False) for i in range(n)], axis)
        x = jnp.where((index & bit) != 0, moved, x)
        bit *= 2
    return x


def norm_forward(resid, gain, shift):
    centre = resid - jnp.mean(resid, axis=-1, keepdims=True)
    factor = lax.rsqrt(jnp.mean(centre * centre, axis=-1, keepdims=True) + epsilon)
    normed = centre * factor
    return (normed * gain + shift, normed, factor)


def norm_backward(grad_out, normed, factor, gain):
    scaled = grad_out * gain
    centred = scaled - jnp.mean(scaled, axis=-1, keepdims=True)
    return factor * (centred - normed * jnp.mean(scaled * normed, axis=-1, keepdims=True))


def on_device(
    tokens,
    cotangent,
    lengths,
    query_weight,
    query_bias,
    key_weight,
    value_weight,
    value_bias,
    out_weight,
    out_bias,
    first_gain,
    first_shift,
    up_weight,
    up_bias,
    down_weight,
    down_bias,
    second_gain,
    second_shift,
):
    shard_n, ctx_n, tp_n = (lax.axis_size(a) for a in ("shard", "ctx", "tp"))
    shard_i, ctx_i, tp_i = (lax.axis_index(a) for a in ("shard", "ctx", "tp"))
    seqs, rows, model = tokens.shape
    part = model // shard_n
    width = query_weight.shape[1]
    heads = width // HD
    units = up_weight.shape[1]
    quarter = units // ctx_n
    two = shard_n == 2
    first = shard_i == 0

    def flip(x):
        if not two:
            return x
        return jnp.where(first, x, jnp.concatenate([x[..., part:], x[..., :part]], -1))

    def gather_local(x):
        if two:
            return jnp.concatenate([x, swap(x, "shard", 1)], -1)
        return lax.all_gather(x, "shard", axis=x.ndim - 1, tiled=True)

    def scatter_local(x):
        if two:
            return wide(x[:, :part]) + wide(swap(x[:, part:], "shard", 1))
        return wide(lax.psum_scatter(x, "shard", scatter_dimension=1, tiled=True))

    def after(x, *gates):
        return lax.optimization_barrier((x, *gates))[0]

    bits = ctx_n.bit_length() - 1
    ctx_bits = [1 << i for i in reversed(range(bits))]

    def bit_reverse(e):
        return sum(((e >> i) & 1) << (bits - 1 - i) for i in range(bits))

    ctx_order = [bit_reverse(e) for e in range(ctx_n)]
    half = (ctx_n + 1) // 2

    def exchange(x):
        return lax.all_to_all(x, "tp", 0, 0, tiled=True)

    def tp_gather(x):
        return exchange(jnp.broadcast_to(x[None], (tp_n, *x.shape)))

    def ctx_gather(chunks, some=None):
        for bit in ctx_bits if some is None else some:
            chunks = chunks + [swap(c, "ctx", bit) for c in chunks]
        return chunks

    kv_t = jnp.stack(
        [key_weight.T.reshape(heads, HD, part), value_weight.T.reshape(heads, HD, part)], 1
    ).reshape(2 * width, part)
    mine = lambda w: lax.dynamic_slice_in_dim(w, ctx_i * quarter, quarter, 0)
    qkv_t = flip(gather_local(jnp.concatenate([query_weight.T, kv_t], 0)))
    kv_bias = jnp.stack(
        [jnp.zeros((heads, HD), f32), value_bias.reshape(heads, HD)], 1
    ).reshape(2 * width, 1)

    first_in = tp_gather(tokens[0])
    blocks = [first_in.reshape(tp_n * rows, model)]
    for s in range(1, seqs):
        blocks.append(tp_gather(after(tokens[s], blocks[-1])).reshape(tp_n * rows, model))

    bias_rows = []
    rest = up_bias
    for _ in range(3):
        bias_rows.append(low(rest))
        rest = rest - wide(bias_rows[-1])
    extra = 3 * units // model
    bias_rows = jnp.stack(bias_rows, 0).reshape(extra, model)
    bias_rows = lax.dynamic_slice_in_dim(bias_rows, shard_i * part, part, 1)
    tail = width // ctx_n // 2
    step = -(-(quarter + tail + extra) // 16) * 16
    out_mine = lax.dynamic_slice_in_dim(out_weight, ctx_i * 2 * tail, 2 * tail, 0)
    fill = jnp.zeros((step - quarter - tail - extra, part), bf16)
    pack = jnp.stack(
        [
            jnp.concatenate([mine(up_weight.T), bias_rows, fill, out_mine[:tail]], 0),
            jnp.concatenate(
                [mine(down_weight), jnp.zeros((extra, part), bf16), fill, out_mine[tail:]], 0
            ),
        ],
        0,
    )
    pack = lax.all_gather(after(pack, blocks[-1]), "tp", axis=1, tiled=True)
    chunk = tp_n * step
    ups = [gather_local(pack[0])]
    downs = after(jnp.concatenate(ctx_gather([pack[1]], ctx_bits[:-1]), 0), *ups)

    place = jnp.arange(ctx_n * tp_n)
    order = bit_reverse((place // tp_n) ^ ctx_i) * tp_n + place % tp_n
    block_at = (bit_reverse(place // tp_n) ^ ctx_i) * tp_n + place % tp_n

    def project(s, block):
        kv = low(dot(qkv_t[width:], block, NT) + kv_bias)
        q = low(dot(qkv_t[:width], block, NT) + query_bias[:, None])
        return kv, q * bf16(HD ** (-0.5))

    def ctx_pieces(kv, gate):
        chunks = [kv]
        for bit in ctx_bits:
            chunks = chunks + [swap(c, "ctx", bit) for c in chunks]
            if gate is not None and bit == ctx_bits[0]:
                chunks = [after(c, gate) for c in chunks]
        return chunks

    metas = []
    for s in range(seqs):
        count = jnp.clip(lengths[s] - block_at * rows, 0, rows)
        metas.append(
            jnp.concatenate([((lengths[s] + rows - 1) // rows)[None], order, count]).astype(
                jnp.int32
            )
        )

    outs, totals, attended, queries, keys_values = [], [], [], [], []
    kv, q = project(0, blocks[0])
    kvs = ctx_pieces(kv, None)
    for s in range(seqs):
        keys_values.append(kvs)
        queries.append(q)
        if s + 1 < seqs and heads > 1:
            ot_a, lse_a = attend_forward(metas[s], q, kvs, rows, 0, heads - 1)
            kv_next, q_next = project(s + 1, after(blocks[s + 1], lse_a))
            meta = after(metas[s], kv_next, q_next)
            ot_b, lse_b = attend_forward(meta, q, kvs, rows, heads - 1, 1)
            ot = jnp.concatenate([ot_a, ot_b], 1)
            lse = jnp.concatenate([lse_a, lse_b], 0)
            q, kvs = q_next, ctx_pieces(kv_next, lse_b)
        else:
            ot_a, lse_a = attend_forward(metas[s], q, kvs, rows, 0, heads - 1)
            meta = after(metas[s], lse_a, ups[0], downs)
            ot_b, lse_b = attend_forward(meta, q, kvs, rows, heads - 1, 1)
            ot = jnp.concatenate([ot_a, ot_b], 1)
            lse = jnp.concatenate([lse_a, lse_b], 0)
        outs.append(ot)
        totals.append(lse)
        attended.append(exchange(ot).reshape(tp_n * width, rows))
    ups = ctx_gather(ups)
    downs = after(gather_local(downs), attended[-1])
    downs = [downs[i * chunk : (i + 1) * chunk] for i in range(half)]
    downs = ctx_gather(downs, ctx_bits[-1:])

    def natural(pieces):
        whole = jnp.zeros((ctx_n, *pieces[0].shape), bf16)
        for e, piece in zip(ctx_order, pieces):
            whole = lax.dynamic_update_slice_in_dim(whole, piece[None], e ^ ctx_i, 0)
        return whole

    ups = [x.reshape(tp_n, step, model) for x in ups]
    downs = [x.reshape(tp_n, step, model) for x in downs]
    up_full = natural([x[:, :quarter] for x in ups]).reshape(-1, model)
    down_full = natural([x[:, :quarter] for x in downs]).reshape(-1, model)
    ends = [
        jnp.stack([x[:, step - tail :] for x in pair], 1) for pair in zip(ups, downs)
    ]
    out_full = natural(ends).transpose(1, 0, 2, 3, 4).reshape(tp_n * width, model)
    unit_bias = wide(flip(ups[0][:, quarter : quarter + extra]))
    unit_bias = unit_bias.reshape(tp_n, 3, ctx_n, quarter)
    unit_bias = (unit_bias[:, 0] + unit_bias[:, 1]) + unit_bias[:, 2]
    unit_bias = unit_bias.transpose(1, 0, 2).reshape(1, ctx_n * tp_n * quarter)

    attended_t = jnp.concatenate(attended, 1)

    flat = flip(wide(tokens.reshape(seqs * rows, model)))
    cot = flip(wide(cotangent.reshape(seqs * rows, model)))
    gain_1, shift_1, gain_2, shift_2, bias_o, bias_d = (
        flip(v) for v in (first_gain, first_shift, second_gain, second_shift, out_bias, down_bias)
    )
    mixed = dot(attended_t, out_full, TN) + bias_o
    hidden, normed_1, factor_1 = norm_forward(flat + mixed, gain_1, shift_1)
    hidden_low = low(hidden)
    pre = dot(hidden_low, up_full, NT) + unit_bias
    share = 0.5 * (1.0 + lax.erf(pre * 0.5**0.5))
    activated = low(pre * share)
    slope = low(share + pre * jnp.exp(-0.5 * pre * pre) * 0.3989422804014327)
    ffn_out = dot(activated, down_full, NN) + bias_d
    result, normed_2, factor_2 = norm_forward(hidden + ffn_out, gain_2, shift_2)
    here = (ctx_i * tp_n + tp_i) * rows + jnp.arange(rows)
    valid = (here[None, :] < lengths[:, None]).reshape(seqs * rows, 1)
    grad_result = jnp.where(valid, cot, 0.0)
    gain_2_grad = jnp.sum(grad_result * normed_2, axis=0)
    shift_2_grad = jnp.sum(grad_result, axis=0)
    grad_second = norm_backward(grad_result, normed_2, factor_2, gain_2)
    ffn_grad = low(grad_second)
    bias_d_grad = jnp.sum(wide(ffn_grad), axis=0)
    pre_grad = low(dot(ffn_grad, down_full, NT) * wide(slope))
    grad_hidden = grad_second + dot(pre_grad, up_full, NN)
    up_bias_grad = jnp.sum(wide(pre_grad), axis=0)
    gain_1_grad = jnp.sum(grad_hidden * normed_1, axis=0)
    shift_1_grad = jnp.sum(grad_hidden, axis=0)
    grad_first = norm_backward(grad_hidden, normed_1, factor_1, gain_1)
    mixer_grad = low(grad_first)
    bias_o_grad = jnp.sum(wide(mixer_grad), axis=0)
    attended_grad_t = low(dot(out_full, mixer_grad, NT))
    value_bias_parts = jnp.sum(
        wide(attended_grad_t).reshape(tp_n, width, seqs * rows), axis=2
    )
    value_bias_grad = value_bias_parts.reshape(-1)
    up_bias_full = up_bias_grad.reshape(ctx_n, tp_n, quarter).transpose(1, 0, 2).reshape(-1)
    up_rows = up_bias_full.shape[0] // model
    vectors = [
        flip(value_bias_grad),
        bias_o_grad,
        gain_1_grad,
        shift_1_grad,
        flip(up_bias_full.reshape(up_rows, model)),
        bias_d_grad,
        gain_2_grad,
        shift_2_grad,
    ]
    vectors = [p for v in vectors for p in v.reshape(-1, model)]
    grad_step = -(-(quarter + tail + (len(vectors) + 1) // 2) // 16) * 16
    spare = grad_step - quarter - tail
    vectors = sum(
        jnp.pad(v[None], ((i, 2 * spare - 1 - i), (0, 0))) for i, v in enumerate(vectors)
    ).reshape(2, spare, model)

    grad_cols = exchange(attended_grad_t.reshape(tp_n, width, seqs * rows))

    def sum_ctx(x):
        for bit in reversed(ctx_bits):
            x = low(x)
            x = wide(x) + wide(swap(x, "ctx", bit))
        return x

    late_pre = after(pre_grad, attended_grad_t)
    ffn_grads = weight_grads(
        late_pre,
        hidden_low,
        activated,
        ffn_grad,
        attended_t,
        mixer_grad,
        vectors,
        ctx_n,
        tp_n,
        grad_step,
        tail,
    )
    ffn_sum = lax.psum_scatter(
        after(ffn_grads, grad_cols), ("ctx", "tp"), scatter_dimension=1, tiled=True
    )

    grad_rows = flip(grad_first).reshape(seqs, rows, model)
    spans = []
    for s in range(seqs):
        if s + 1 < seqs or heads == 1:
            spans.append((s, 0, heads))
        else:
            spans += [(s, 0, 1), (s, 1, heads - 1)]
    near = ctx_bits[-1:]
    far = list(reversed(ctx_bits[:-1]))

    def near_sum(keep, send):
        got = send
        for bit in near:
            got = swap(send, "ctx", bit)
        return [(keep[p], got[p]) if p == 0 else low(wide(keep[p]) + wide(got[p])) for p in range(half)]

    def far_sum(chunks):
        first, rest = chunks[0], chunks[1:]
        total = wide(first[0]) + wide(first[1])
        if len(far) == 1:
            return low(total + wide(swap(rest[0], "ctx", far[0])))
        chunks = [low(total)] + rest
        for bit in far:
            n = len(chunks) // 2
            chunks = [
                low(wide(a) + wide(swap(b, "ctx", bit))) for a, b in zip(chunks[:n], chunks[n:])
            ]
        return chunks[0]

    qkv_grad = 0.0
    sums = 0.0
    dq_parts = [[] for _ in range(seqs)]
    dkv_parts = [[] for _ in range(seqs)]
    last = ()
    near_chunks = None
    number = 0

    def finish(s, *gates):
        grads_t = jnp.concatenate(dq_parts[s] + dkv_parts[s], 0)
        back = low(dot(grads_t, qkv_t, TN))
        if gates:
            back = after(back, *gates)
        cut = back.reshape(tp_n, rows, model)
        if s + 1 < seqs:
            total = [lax.dynamic_index_in_dim(cut, tp_i, 0, False)] + [
                swap(lax.dynamic_index_in_dim(cut, tp_i ^ j, 0, False), "tp", j)
                for j in range(1, tp_n)
            ]
        else:
            total = [lax.psum_scatter(back, "tp", scatter_dimension=0, tiled=True)]
        return (
            back,
            total,
            dot(after(grads_t, back), blocks[s], NN),
            jnp.sum(wide(jnp.concatenate(dq_parts[s], 0)), axis=1),
        )

    def received(s, parts):
        total = grad_rows[s]
        for p in parts:
            total = total + wide(p)
        return low(total)

    moving = {}
    for s, start, count in spans:
        meta = metas[s]
        wait = list(last) if last else [grad_cols]
        if number >= 1:
            wait += near_chunks[1:]
        if number >= 2:
            done_s = spans[number - 2][0]
            wait.append(dkv_parts[done_s][-1])
            if spans[number - 1][0] != done_s:
                done = finish(done_s)
                wait.append(done[0])
                moving[done_s] = done[1]
                qkv_grad, sums = qkv_grad + done[2], sums + done[3]
        if wait:
            meta = after(meta, *wait)
        dq, keep, send = attend_backward(
            meta, queries[s], outs[s], grad_cols, totals[s], keys_values[s], rows, start, count, s
        )
        last = (dq,)
        number += 1
        if number > 1:
            before = spans[number - 2][0]
            keep, send, dkv_parts[before][-1] = lax.optimization_barrier(
                (keep, send, dkv_parts[before][-1])
            )
            for parts in moving.values():
                keep, send, parts[1:] = lax.optimization_barrier((keep, send, parts[1:]))
        near_chunks = near_sum(keep, send)
        dq_parts[s].append(dq)
        dkv_parts[s].append(far_sum(near_chunks))
    ffn_sum = low(scatter_local(ffn_sum.reshape(2 * grad_step, model)))
    done = finish(seqs - 1)
    moving[seqs - 1] = done[1]
    qkv_grad, sums = qkv_grad + done[2], sums + done[3]
    chunks = ctx_gather([ffn_sum])
    stacked = jnp.stack([chunks[ctx_order.index(e)] for e in range(ctx_n)], 0)
    stacked = xor_order(stacked, 0, ctx_i).reshape(ctx_n, 2, grad_step, part)
    summed = stacked[0, :, quarter + tail :].reshape(2 * spare, part)
    for i in range(tp_n.bit_length() - 1):
        summed = jnp.where((tp_i >> i) & 1 != 0, swap(summed, "tp", 1 << i), summed)
    summed = wide(flip(gather_local(summed)))
    stacked = wide(stacked)
    up_sum = stacked[:, 0, :quarter].reshape(units, part)
    down_sum = stacked[:, 1, :quarter].reshape(units, part)
    out_sum = stacked[:, :, quarter : quarter + tail].reshape(width, part)

    if two:
        sums = jnp.pad(sums, (0, part - width))
        sums = jnp.pad(jnp.concatenate([sums, sums])[None], ((0, 15), (0, 0)))
        qkv_sum = scatter_local(flip(low(jnp.concatenate([qkv_grad, sums], 0))))
        qkv_sum = sum_ctx(qkv_sum)
        query_bias_sum = qkv_sum[3 * width, :width]
    else:
        qkv_sum = sum_ctx(scatter_local(low(qkv_grad)))
        query_bias_sum = lax.psum(sums, ("shard", "ctx"))
    query_sum = qkv_sum[:width]
    kv_sum = qkv_sum[width : 3 * width].reshape(heads, 2, HD, part)
    key_sum = kv_sum[:, 0].reshape(width, part)
    value_sum = kv_sum[:, 1].reshape(width, part)

    query_bias_parts = [query_bias_sum] + [swap(query_bias_sum, "tp", j) for j in range(1, tp_n)]
    query_bias_full = xor_order(jnp.stack(query_bias_parts, 0), 0, tp_i).reshape(-1)
    moving[seqs - 1][0] = after(moving[seqs - 1][0], query_bias_full, qkv_sum, out_sum, summed)
    input_grads = jnp.stack([received(s, moving[s]) for s in range(seqs)], 0)
    ends = [*summed[:4], summed[4 : 4 + up_rows].reshape(-1), *summed[4 + up_rows : 7 + up_rows]]
    return (
        low(flip(result)).reshape(seqs, rows, model),
        input_grads,
        query_sum.T,
        query_bias_full,
        key_sum.T,
        value_sum.T,
        ends[0],
        out_sum,
        ends[1],
        ends[2],
        ends[3],
        up_sum.T,
        ends[4],
        down_sum,
        ends[5],
        ends[6],
        ends[7],
    )


def solution(mesh):
    placed = (
        P("shard", ("ctx", "tp"), None),
        P("shard", ("ctx", "tp"), None),
        P("shard"),
        P("shard", "tp"),
        P("tp"),
        P("shard", "tp"),
        P("shard", "tp"),
        P("tp"),
        P("tp", "shard"),
        P(),
        P(),
        P(),
        P("shard", "tp"),
        P("tp"),
        P("tp", "shard"),
        P(),
        P(),
        P(),
    )
    return jax.shard_map(
        on_device,
        mesh=mesh,
        in_specs=placed,
        out_specs=(
            P("shard", ("ctx", "tp"), None),
            P("shard", ("ctx", "tp"), None),
            P("shard", "tp"),
            P(),
            P("shard", "tp"),
            P("shard", "tp"),
            P(),
            P("tp", "shard"),
            P(),
            P(),
            P(),
            P("shard", "tp"),
            P(),
            P("tp", "shard"),
            P(),
            P(),
            P(),
        ),
        check_vma=False,
    )
```
